1024 devices in a mesh: gx: 64 (over z, y_hi, core), gy: 16 (over x, y_lo).
Axes of the slice: x: 4, y: 8 (y_hi: 2, y_lo: 4; y = y_hi * 4 + y_lo), z: 16, core: 2. Of those that a mesh axis runs over, the one named last changes fastest.
Arguments:
- orbitals: bfloat16 [351232, 512], P(('gx', 'gy')), may hold values from -24 to 24
- potential: float32 [351232], P(('gx', 'gy')), may hold values from 0.5 to 2
- cell_stiffness: bfloat16 [512, 512], replicated, may hold values from -1 to 2.5, as said below
Outputs:
- filtered: bfloat16 [351232, 512], P(('gx', 'gy'))
- projected_ham: float32 [512, 512], P('gx', 'gy')
- correlation: float32 [512, 512], P('gx', 'gy')
The draws below stay inside these ranges and needn't reach their ends.
Inputs may be any that keep to these rules, and one draw needn't show every extreme that they name: `cell_stiffness`: symmetric.
All inputs are finite; a program needn't handle non-finite values.
Results may differ from the reference program's by a relative error of at most 0.005.
Values may be sent and summed in bfloat16 or wider, within the bound.
No kernel may reach another device: no remote copies, remote signals or barrier semaphores. Data moves between devices by JAX's collectives and lax.ppermute only.
A program may use at most 32 MiB of HBM per device.

```python
import math
import jax
import jax.numpy as jnp
from jax import lax

NORB = 512
DEG = 7
CZ = 1
NPC = 512
NODES = 351232
N_GX = 64
N_GY = 16


def draw_cell_stiffness(key, part):
    key_noise, key_diag = jax.random.split(jax.random.fold_in(key, 11))
    noise_draw = jnp.clip(jax.random.normal(key_noise, (NPC, NPC), jnp.float32), -5.0, 5.0)
    symmetric = (noise_draw + noise_draw.T) * (0.5 / math.sqrt(2.0 * NPC))
    diagonal = jax.random.uniform(key_diag, (NPC,), jnp.float32, 0.5, 1.5)
    return (symmetric + jnp.diag(diagonal)).astype(jnp.bfloat16)


def spiked(values, own_key, source, target, blocks, factor):
    def block_of(dim):
        return (jnp.arange(values.shape[dim]) // (values.shape[dim] // blocks)).reshape((-1,) + (1,) * (values.ndim - 1 - dim))

    one_side = jax.random.permutation(own_key, blocks)[block_of(target)]
    second = (block_of(target) + blocks // 2) % blocks
    return jnp.where((block_of(source) == one_side) | (block_of(source) == second), factor * values, values)


def shard_levels(stream_key, shape, pieces, smallest, largest):
    level, own = 1.0, jax.random.fold_in(stream_key, 6)
    for position, parts in pieces:
        steps = jnp.exp(jax.random.uniform(jax.random.fold_in(own, position), (parts,), jnp.float32, smallest / len(pieces), largest / len(pieces)))
        level = level * jnp.repeat(steps, shape[position] // parts).reshape([-1 if axis == position else 1 for axis in range(len(shape))])
    return level


def bell_draw_with(own_key, extent, scale, limit, cuts, heavy, kind=jnp.bfloat16):
    drawn = scale * jax.random.normal(own_key, extent, jnp.float32)
    if cuts:
        drawn = drawn * shard_levels(own_key, extent, cuts, -0.22, 0.18)
    return jnp.clip(spiked(drawn, jax.random.fold_in(own_key, 3), *heavy), -limit, limit).astype(kind)


def setup_inputs(seed: int = 0) -> dict:
    arg_keys = jax.random.split(jax.random.key(seed), 4)
    orbitals = bell_draw_with(arg_keys[0], (NODES, NORB), 1.0, 24.0, ((0, 1024),), (0, 1, 512, 6.0))
    potential = jnp.clip(0.5 + 1.5 * jax.random.uniform(arg_keys[1], (NODES,), jnp.float32) ** shard_levels(arg_keys[1], (NODES,), ((0, 1024),), -0.2, 0.2), 0.5, 2.0)
    cell_stiffness = draw_cell_stiffness(jax.random.fold_in(arg_keys[3], 71), 0)
    return {"orbitals": orbitals, "potential": potential, "cell_stiffness": cell_stiffness}


SPECTRUM_CENTER = 2.0
SPECTRUM_HALF = 2.0

def split_axis(values, which, degree):
    length = values.shape[which]
    cell_count = (length - 1) // degree
    leading = lax.slice_in_dim(values, 0, degree * cell_count, axis=which)
    leading = leading.reshape(values.shape[:which] + (cell_count, degree) + values.shape[which + 1:])
    trailing = lax.slice_in_dim(values, degree, length, stride=degree, axis=which)
    trailing = jnp.expand_dims(trailing, which + 1)
    joined = jnp.concatenate([leading, trailing], axis=which + 1)
    return jnp.swapaxes(joined, which, which + 1)

def join_axis(values, which, degree):
    values = jnp.swapaxes(values, which, which + 1)
    cell_count = values.shape[which]
    new_shape = values.shape[:which] + (cell_count * degree,) + values.shape[which + 2:]
    leading = lax.slice_in_dim(values, 0, degree, axis=which + 1).reshape(new_shape)
    trailing = lax.slice_in_dim(values, degree, degree + 1, axis=which + 1)
    filler = jnp.zeros(trailing.shape[:which + 1] + (degree - 1,) + trailing.shape[which + 2:], values.dtype)
    trailing = jnp.concatenate([filler, trailing], axis=which + 1).reshape(new_shape)
    widths_lead = [(0, 0)] * len(new_shape)
    widths_lead[which] = (0, 1)
    widths_trail = [(0, 0)] * len(new_shape)
    widths_trail[which] = (1, 0)
    return jnp.pad(leading, widths_lead) + jnp.pad(trailing, widths_trail)

def cell_image(node_slab, stiffness_rows, degree):
    side = degree + 1
    cells = split_axis(node_slab, 1, degree)
    cells = split_axis(cells, 3, degree)
    cells = jnp.transpose(cells, (0, 1, 3, 2, 4, 5))
    cell_shape = cells.shape
    product = jnp.dot(stiffness_rows, cells.reshape(side ** 3, -1), preferred_element_type=jnp.float32)
    product = product.reshape((stiffness_rows.shape[0] // (side * side),) + cell_shape[1:])
    product = jnp.transpose(product, (0, 1, 3, 2, 4, 5))
    product = join_axis(product, 3, degree)
    return join_axis(product, 1, degree)

def gram(left, right):
    return lax.dot_general(left, right, (((0,), (0,)), ((), ())), preferred_element_type=jnp.float32)

def reference(orbitals, potential, cell_stiffness):
    plane_z = DEG * CZ
    plane_y = DEG * N_GY
    side = DEG + 1
    total_nodes = DEG * DEG * plane_z * N_GX * N_GY
    norm_scale = 1.0 / math.sqrt(total_nodes)
    field_six = orbitals.reshape(N_GX, N_GY, DEG, DEG, plane_z, NORB)
    potential_six = potential.reshape(N_GX, N_GY, DEG, DEG, plane_z)
    top_rows = cell_stiffness[DEG * side * side:]

    def to_slab(device_block):
        swapped = jnp.swapaxes(device_block, 0, 1)
        return swapped.reshape((DEG, plane_y) + swapped.shape[3:])

    def from_slab(node_slab):
        swapped = node_slab.reshape((DEG, N_GY, DEG) + node_slab.shape[2:])
        return jnp.swapaxes(swapped, 0, 1)

    def build_slab(field, slab_index):
        owned = to_slab(lax.dynamic_index_in_dim(field, slab_index, 0, keepdims=False))
        next_index = jnp.minimum(slab_index + 1, N_GX - 1)
        next_plane = to_slab(lax.dynamic_index_in_dim(field, next_index, 0, keepdims=False))[0:1]
        next_plane = jnp.where(slab_index + 1 < N_GX, next_plane, jnp.zeros_like(next_plane))
        node_slab = jnp.concatenate([owned, next_plane], axis=0)
        node_slab = jnp.pad(node_slab, ((0, 0), (0, 1), (0, 1), (0, 0)))
        return (owned, node_slab)

    def slab_image(field, slab_index):
        owned, node_slab = build_slab(field, slab_index)
        contrib = cell_image(node_slab, cell_stiffness, DEG)
        lower_index = jnp.maximum(slab_index - 1, 0)
        _, lower_slab = build_slab(field, lower_index)
        lower_top = cell_image(lower_slab, top_rows, DEG)[0, :plane_y, :plane_z]
        lower_top = jnp.where(slab_index > 0, lower_top, jnp.zeros_like(lower_top))
        interior = contrib[:DEG, :plane_y, :plane_z]
        interior = jnp.concatenate([interior[0:1] + lower_top[None], interior[1:]], axis=0)
        potential_slab = to_slab(lax.dynamic_index_in_dim(potential_six, slab_index, 0, keepdims=False))
        image = interior + potential_slab[..., None] * owned.astype(jnp.float32)
        return (image, owned)
    indices = jnp.arange(N_GX, dtype=jnp.int32)

    def first_pass(slab_index):
        image, owned = slab_image(field_six, slab_index)
        lifted = ((image - SPECTRUM_CENTER * owned.astype(jnp.float32)) / SPECTRUM_HALF).astype(jnp.bfloat16)
        return from_slab(lifted)
    lifted_six = lax.map(first_pass, indices)

    def second_pass(state, slab_index):
        ham_acc, correlation_acc = state
        image, owned = slab_image(lifted_six, slab_index)
        initial = to_slab(lax.dynamic_index_in_dim(field_six, slab_index, 0, keepdims=False))
        filtered = (2.0 * (image - SPECTRUM_CENTER * owned.astype(jnp.float32)) / SPECTRUM_HALF - initial.astype(jnp.float32)).astype(jnp.bfloat16)
        image_rounded = image.astype(jnp.bfloat16)
        ham_acc = ham_acc + gram(owned.reshape(-1, NORB), image_rounded.reshape(-1, NORB))
        flat_filtered = filtered.reshape(-1, NORB)
        correlation_acc = correlation_acc + gram(flat_filtered, flat_filtered)
        return ((ham_acc, correlation_acc), from_slab(filtered))
    zeros_square = jnp.zeros((NORB, NORB), jnp.float32)
    final_state, filtered_six = lax.scan(second_pass, (zeros_square, zeros_square), indices)
    ham_acc, correlation_acc = final_state
    return (filtered_six.reshape(total_nodes, NORB), ham_acc * norm_scale, correlation_acc * norm_scale)
```

```python
import math

import numpy as np

import jax
import jax.numpy as jnp
from jax import lax
from jax.experimental import pallas as pl
from jax.experimental.pallas import tpu as pltpu
from jax.sharding import Mesh, PartitionSpec as P

DEG = 7
SIDE = DEG + 1
FACE = DEG * DEG
RIM = FACE + DEG
OWN = FACE * DEG
CELL = OWN + 2 * FACE + DEG
VMEM_LIMIT = 24 * 2**20
SPECTRUM_CENTER = 2.0
SPECTRUM_HALF = 2.0
F32 = jnp.float32
BF16 = jnp.bfloat16


def node_lists():
    def at(a, b):
        return [(a * SIDE + b) * SIDE + c for c in range(DEG)]

    own = [n for a in range(DEG) for b in range(DEG) for n in at(a, b)]
    face_x = [n for b in range(DEG) for n in at(DEG, b)]
    face_y = [n for a in range(DEG) for n in at(a, DEG)]
    return own, face_x, face_y, at(DEG, DEG)


def dot(left, right):
    return jnp.dot(left, right, preferred_element_type=F32)


def gram(left, right):
    return lax.dot_general(left, right, (((0,), (0,)), ((), ())), preferred_element_type=F32)


def one_hot(column, width):
    return (column == lax.broadcasted_iota(jnp.int32, (column.shape[0], width), 1)).astype(F32).astype(BF16)


def call(kernel, *shapes, scratch=(), results=()):
    def run(*args):
        vmem = pl.BlockSpec(memory_space=pltpu.VMEM)
        return pl.pallas_call(
            kernel,
            out_shape=[
                jax.ShapeDtypeStruct(*shape) if i in results else pltpu.VMEM(*shape) for i, shape in enumerate(shapes)
            ],
            in_specs=[vmem] * len(args),
            out_specs=[vmem] * len(shapes),
            scratch_shapes=list(scratch),
            compiler_params=pltpu.CompilerParams(vmem_limit_bytes=VMEM_LIMIT),
            name=kernel.__name__,
        )(*[pltpu.with_memory_space_constraint(arg, pltpu.VMEM) for arg in args])

    return run


def take_face_y(source, packed):
    for i in range(DEG):
        packed[i * DEG : (i + 1) * DEG, :] = source[i * FACE : i * FACE + DEG, :]


def prepare_body(field, stiffness, rows, columns, order_out, face_y, partial, wide, packed):
    left = one_hot(rows[...], SIDE**3)
    right = one_hot(columns[...], SIDE**3)
    mixed = dot(left, stiffness[...]).astype(BF16)
    order_out[...] = lax.dot_general(mixed, right, (((1,), (1,)), ((), ())), preferred_element_type=F32).astype(BF16)
    wide[...] = field[...].astype(F32)
    take_face_y(wide, packed)
    face_y[...] = packed[...].astype(BF16)
    partial[...] = dot(order_out[:, :OWN], field[...])


def add_face_body(ordered, partial, face_x, total):
    total[...] = partial[...] + dot(ordered[:, OWN : OWN + FACE], face_x[...])


def close_body(ordered, partial, rim, own, away_x, face_y):
    total = partial[...] + dot(ordered[:, OWN + FACE :], rim[...])
    own[...] = total[:OWN]
    away_x[...] = total[OWN : OWN + RIM]
    face_y[...] = total[OWN + RIM :]


def lift_body(own, from_x, from_y, field, potential, lifted, face_x, face_y, image, packed):
    field32 = field[...].astype(F32)
    image[...] = own[...]
    image[:FACE, :] += from_x[:FACE, :]
    for i in range(DEG):
        image[i * FACE : i * FACE + DEG, :] += from_y[i * DEG : (i + 1) * DEG, :]
    first_image = image[...] + potential[...] * field32
    image[...] = (first_image - SPECTRUM_CENTER * field32) / SPECTRUM_HALF
    lifted[...] = image[...].astype(BF16)
    face_x[...] = image[:FACE, :].astype(BF16)
    take_face_y(image, packed)
    face_y[...] = packed[...].astype(BF16)


def multiply_body(ordered, lifted, partial):
    partial[...] = dot(ordered[:, :OWN], lifted[...])


def solution(mesh):
    length_x, length_y = mesh.shape["gx"], mesh.shape["gy"]
    length_z = length_x // 4
    split_mesh = Mesh(mesh.devices.reshape(length_z, 2, 2, length_y), ("z", "half", "core", "gy"))
    gx = ("z", "half", "core")
    every = gx + ("gy",)

    def passed_x(value, by):
        return lax.ppermute(value, gx, [(i, i + by) for i in range(length_x) if 0 <= i + by < length_x])

    def passed_y(value, by):
        return lax.ppermute(value, "gy", [(i, i + by) for i in range(length_y) if 0 <= i + by < length_y])

    def per_device(orbitals, potential, cell_stiffness):
        node_count, orbital_count = orbitals.shape
        norm_scale = 1.0 / math.sqrt(node_count * length_x * length_y)
        block_rows = orbital_count // length_x
        block_cols = orbital_count // length_y
        half = orbital_count // 2
        quarter = orbital_count // 4
        own, face_x, face_y, edge = node_lists()
        row_order = jnp.asarray(np.array(own + face_x + edge + face_y, np.int32)[:, None])
        column_order = jnp.asarray(np.array(own + face_x + face_y + edge, np.int32)[:, None])
        orbital_order = jnp.asarray(
            np.arange(orbital_count, dtype=np.int32)
            .reshape(length_z, 2, 2, block_rows)
            .transpose(2, 1, 0, 3)
            .reshape(-1, 1)
        )
        weight = potential[:, None]
        face = (FACE, orbital_count)
        cell = (CELL, orbital_count)
        nodes = (OWN, orbital_count)
        rim = (RIM, orbital_count)

        def closed(ordered, partial, above_x, own_face_y):
            total = call(add_face_body, (cell, F32))(ordered, partial, above_x)[0]
            above_y = passed_y(jnp.concatenate([own_face_y, above_x[:DEG]], axis=0), -1)
            return above_y, *call(close_body, (nodes, F32), (rim, F32), (face, F32))(ordered, total, above_y)

        def shared(away_x, away_y):
            from_x = passed_x(away_x, 1)
            from_y = passed_y(away_y + jnp.pad(from_x[FACE:], ((0, FACE - DEG), (0, 0))), 1)
            return from_x, from_y

        above_x = passed_x(orbitals[:FACE], -1)
        ordered, own_face_y, partial = call(
            prepare_body,
            ((CELL, CELL), BF16),
            (face, BF16),
            (cell, F32),
            scratch=(pltpu.VMEM(nodes, F32), pltpu.VMEM(face, F32)),
        )(orbitals, cell_stiffness, row_order, column_order)
        _, own_image, away_x, away_y = closed(ordered, partial, above_x, own_face_y)
        from_x, from_y = shared(away_x, away_y)
        lifted, lifted_face_x, lifted_face_y = call(
            lift_body,
            (nodes, BF16),
            (face, BF16),
            (face, BF16),
            scratch=(pltpu.VMEM(nodes, F32), pltpu.VMEM(face, F32)),
        )(own_image, from_x, from_y, orbitals, weight)

        above_x = passed_x(lifted_face_x, -1)
        partial = call(multiply_body, (cell, F32))(ordered, lifted)[0]
        above_y, own_image, away_x, away_y = closed(ordered, partial, above_x, lifted_face_y)
        from_x, from_y = shared(away_x, away_y)

        gram_shape = (2, orbital_count, half)
        padded = -(-CELL // 128) * 128

        def ham_body(own_image, away_x, away_y, lifted, above_x, above_y, potential, order, out, images, values):
            values[CELL:, :] = jnp.zeros((padded - CELL, orbital_count), F32)
            images[CELL:, :] = jnp.zeros((padded - CELL, orbital_count), F32)
            values[:OWN, :] = lifted[...].astype(F32)
            values[OWN : OWN + FACE, :] = above_x[...].astype(F32)
            values[OWN + FACE : CELL, :] = above_y[...].astype(F32)
            images[:OWN, :] = own_image[...] + potential[...] * values[:OWN, :]
            images[OWN : OWN + FACE, :] = away_x[:FACE, :]
            images[OWN + FACE : OWN + 2 * FACE, :] = away_y[...]
            images[OWN + 2 * FACE : CELL, :] = away_x[FACE:, :]
            shuffle = one_hot(order[...], orbital_count)
            shuffled = lax.dot_general(
                values[...].astype(BF16), shuffle, (((1,), (1,)), ((), ())), preferred_element_type=F32
            ).astype(BF16)
            product = (gram(images[...].astype(BF16), shuffled) * norm_scale).astype(BF16)
            out[0] = product[:, :half]
            out[1] = product[:, half:]

        ham_term = call(
            ham_body,
            (gram_shape, BF16),
            scratch=(pltpu.VMEM((padded, orbital_count), F32), pltpu.VMEM((padded, orbital_count), F32)),
        )(own_image, away_x, away_y, lifted, above_x, above_y, weight, orbital_order)[0]

        rows = -(-OWN // 128) * 128

        def filter_body(own_image, from_x, from_y, lifted, field, potential, order, ham, filtered, out, image):
            lifted32 = lifted[...].astype(F32)
            image[OWN:, :] = jnp.zeros((rows - OWN, orbital_count), F32)
            image[:OWN, :] = own_image[...]
            image[:FACE, :] += from_x[:FACE, :]
            for i in range(DEG):
                image[i * FACE : i * FACE + DEG, :] += from_y[i * DEG : (i + 1) * DEG, :]
            second_image = image[:OWN, :] + potential[...] * lifted32
            image[:OWN, :] = (
                2.0 * (second_image - SPECTRUM_CENTER * lifted32) / SPECTRUM_HALF - field[...].astype(F32)
            )
            values = image[...].astype(BF16)
            filtered[...] = image[:OWN, :].astype(BF16)
            shuffle = one_hot(order[...], orbital_count)
            shuffled = lax.dot_general(
                values, shuffle, (((1,), (1,)), ((), ())), preferred_element_type=F32
            ).astype(BF16)
            product = (gram(values, shuffled) * norm_scale).astype(BF16)
            for side in range(2):
                out[side, 0] = ham[side]
                out[side, 1] = product[:, side * half : (side + 1) * half]

        filtered, terms = call(
            filter_body,
            (nodes, BF16),
            ((2, 2, orbital_count, half), BF16),
            scratch=(pltpu.VMEM((rows, orbital_count), F32),),
            results=(0,),
        )(own_image, from_x, from_y, lifted, orbitals, weight, orbital_order, ham_term)

        def pair_body(terms, out):
            for which in range(2):
                total = (terms[0, which].astype(F32) + terms[1, which].astype(F32)).astype(BF16)
                for side in range(2):
                    part = total[:, side * quarter : (side + 1) * quarter]
                    for j in range(length_y):
                        out[side, j, which * block_cols : (which + 1) * block_cols] = part[
                            j * block_cols : (j + 1) * block_cols
                        ]

        def plane_body(terms, out):
            total = terms[0].astype(F32)
            for source in range(1, 2 * length_y):
                total += terms[source].astype(F32)
            out[...] = total.T

        def line_body(terms, ham, correlation):
            total = terms[0]
            for source in range(1, length_z):
                total += terms[source]
            ham[...] = total[:, :block_cols]
            correlation[...] = total[:, block_cols:]

        terms = lax.all_to_all(terms, "core", 0, 0, tiled=True)
        terms = call(pair_body, ((2, length_y, 2 * block_cols, quarter), BF16))(terms)[0]
        terms = terms.reshape(2 * length_y, 2 * block_cols, quarter)
        terms = lax.all_to_all(terms, ("half", "gy"), 0, 0, tiled=True)
        terms = call(plane_body, ((quarter, 2 * block_cols), F32))(terms)[0]
        terms = terms.reshape(length_z, block_rows, 2 * block_cols)
        terms = lax.all_to_all(terms, "z", 0, 0, tiled=True)
        block = (block_rows, block_cols)
        projected_ham, correlation = call(line_body, (block, F32), (block, F32), results=(0, 1))(terms)
        return filtered, projected_ham, correlation

    return jax.shard_map(
        per_device,
        mesh=split_mesh,
        in_specs=(P(every, None), P(every), P()),
        out_specs=(P(every, None), P(gx, "gy"), P(gx, "gy")),
        check_vma=False,
    )
```

```python
import math

import jax
import jax.numpy as jnp
from jax import lax
from jax.experimental import pallas as pl
from jax.experimental.pallas import tpu as pltpu
from jax.sharding import Mesh, PartitionSpec as P

DEG = 7
SIDE = DEG + 1
FACE = DEG * DEG
RIM = FACE + DEG
OWN = FACE * DEG
CELL = OWN + RIM + FACE
SPECTRUM_CENTER = 2.0
SPECTRUM_HALF = 2.0
VMEM_LIMIT = 24 * 2**20
F32 = jnp.float32
BF16 = jnp.bfloat16


def dot(left, right):
    return jnp.dot(left, right, preferred_element_type=F32)


def dot_rows(left, right):
    return lax.dot_general(left, right, (((0,), (0,)), ((), ())), preferred_element_type=F32)


def dot_columns(left, right):
    return lax.dot_general(left, right, (((1,), (1,)), ((), ())), preferred_element_type=F32)


def one_hot(column, width):
    return (column == lax.broadcasted_iota(jnp.int32, (column.shape[0], width), 1)).astype(F32).astype(BF16)


def node_order():
    place = lax.broadcasted_iota(jnp.int32, (CELL, 1), 0)

    def seventh(n):
        return lax.shift_right_logical(n * 9363, 16)

    column = seventh(place)
    plane = seventh(column)
    own = plane * SIDE * SIDE + (column - plane * DEG) * SIDE + (place - column * DEG)
    rim = place - OWN
    rim = DEG * SIDE * SIDE + seventh(rim) * SIDE + (rim - seventh(rim) * DEG)
    face = place - OWN - RIM
    face = seventh(face) * SIDE * SIDE + DEG * SIDE + (face - seventh(face) * DEG)
    return jnp.where(place < OWN, own, jnp.where(place < OWN + RIM, rim, face))


def call(kernel, *shapes, scratch=(), results=(), raw=(), scalar=()):
    def run(*args):
        vmem = pl.BlockSpec(memory_space=pltpu.VMEM)
        places = [
            pl.BlockSpec(memory_space=pl.ANY)
            if i in raw
            else pl.BlockSpec(memory_space=pltpu.SMEM)
            if i in scalar
            else vmem
            for i in range(len(args))
        ]
        return pl.pallas_call(
            kernel,
            out_shape=[
                jax.ShapeDtypeStruct(*shape) if i in results else pltpu.VMEM(*shape) for i, shape in enumerate(shapes)
            ],
            in_specs=places,
            out_specs=[vmem] * len(shapes),
            scratch_shapes=list(scratch),
            compiler_params=pltpu.CompilerParams(vmem_limit_bytes=VMEM_LIMIT),
            name=kernel.__name__,
        )(
            *[
                arg
                if i in scalar
                else pltpu.with_memory_space_constraint(arg, pltpu.HBM if i in raw else pltpu.VMEM)
                for i, arg in enumerate(args)
            ]
        )

    return run


def pack_upward(partial, wide, message, stage):
    rim = partial[OWN : OWN + RIM, :]
    high = rim.astype(BF16).astype(F32)
    stage[:RIM, :] = high
    stage[RIM : 2 * RIM, :] = rim - high
    for i in range(DEG):
        stage[2 * RIM + i * DEG : 2 * RIM + (i + 1) * DEG, :] = wide[i * FACE : i * FACE + DEG, :]
    message[...] = stage[...].astype(BF16)


def prepare(field_in, stiffness_in, field, ordered, own_columns, partial, message, stiffness, wide, stage, sems):
    copies = [
        pltpu.make_async_copy(stiffness_in, stiffness, sems.at[0]),
        pltpu.make_async_copy(field_in, field, sems.at[1]),
    ]
    for copy in copies:
        copy.start()
    order = one_hot(node_order(), SIDE**3)
    copies[0].wait()
    ordered[...] = dot_columns(dot(order, stiffness[...]).astype(BF16), order)
    own_columns[...] = ordered[:, :OWN].astype(BF16)
    copies[1].wait()
    partial[...] = dot(own_columns[...], field[...])
    wide[...] = field[...].astype(F32)
    pack_upward(partial, wide, message, stage)


def split_matrix(ordered, own_x, rim_x, face_x, own_y, side_y, face_y, edge_y):
    to_x, to_y = OWN, OWN + FACE
    own_x[...] = ordered[:OWN, to_x:to_y].astype(BF16)
    rim_x[...] = ordered[OWN : OWN + RIM, to_x:to_y].astype(BF16)
    face_x[...] = ordered[OWN + RIM :, to_x:to_y].astype(BF16)
    own_y[...] = ordered[:OWN, to_y:].astype(BF16)
    side_y[...] = ordered[OWN : OWN + FACE, to_y:].astype(BF16)
    face_y[...] = ordered[OWN + RIM :, to_y:].astype(BF16)
    edge_y[...] = ordered[OWN + FACE : OWN + RIM, to_y:].astype(BF16)


def cross(inside, rim_x, face_x, partial, field, above_x, message, upward, downward, rim, wide, face, stage):
    wide[...] = message[...].astype(F32)
    rim[...] = wide[:RIM, :] + wide[RIM : 2 * RIM, :] + inside[0] * dot(rim_x[...], field[:FACE, :])
    upward[...] = partial[OWN + RIM :, :] + dot(face_x[...], above_x[...])
    upward[:DEG, :] += rim[FACE:, :]
    face[...] = above_x[...].astype(F32)
    stage[:DEG, :] = face[:DEG, :]
    own = field[...].astype(F32)
    for i in range(DEG):
        stage[DEG + i * DEG : DEG + (i + 1) * DEG, :] = own[i * FACE : i * FACE + DEG, :]
    stage[RIM:, :] = wide[2 * RIM :, :]
    downward[...] = stage[...].astype(BF16)


def gather_row(inside, own_x, face_y, edge_y, partial, field, above_x, rim, downward, own, corner, face):
    own[...] = partial[:OWN, :] + dot(own_x[...], above_x[...])
    own[:FACE, :] += rim[:FACE, :]
    face[...] = inside[1] * dot(face_y[...], downward[:RIM, :])
    for i in range(DEG):
        own[i * FACE : i * FACE + DEG, :] += face[i * DEG : (i + 1) * DEG, :]
    wide = downward[...].astype(F32)
    corner[:DEG, :] = field[...].astype(F32)[:DEG]
    corner[DEG:, :] = wide[RIM:]
    own[:DEG, :] += inside[0] * inside[1] * dot(edge_y[...], corner[...].astype(BF16))


def close(inside, own_y, side_y, own, from_y, above_y, image, far):
    wide = above_y[...].astype(F32)
    far[:DEG, :] = wide[DEG : 2 * DEG]
    far[DEG:, :] = wide[RIM:]
    image[:OWN, :] = own[...] + dot(own_y[...], above_y[:RIM, :])
    image[:FACE, :] += inside[0] * dot(side_y[...], far[...].astype(BF16))
    for i in range(DEG):
        image[i * FACE : i * FACE + DEG, :] += from_y[i * DEG : (i + 1) * DEG, :]


def lift(
    inside, own_y, side_y, own, from_y, above_y, field, potential, own_columns,
    lifted, partial, lowest, message, image, far, stage,
):
    close(inside, own_y, side_y, own, from_y, above_y, image, far)
    field32 = field[...].astype(F32)
    first_image = image[...] + potential[...] * field32
    image[...] = (first_image - SPECTRUM_CENTER * field32) / SPECTRUM_HALF
    lifted[...] = image[...].astype(BF16)
    lowest[...] = image[:FACE, :].astype(BF16)
    partial[...] = dot(own_columns[...], lifted[...])
    pack_upward(partial, image, message, stage)


def solution(mesh):
    length_x, length_y = mesh.shape["gx"], mesh.shape["gy"]
    length_z = length_x // 4
    split_mesh = Mesh(mesh.devices.reshape(length_z, 2, 2, length_y), ("z", "half", "core", "gy"))
    gx = ("z", "half", "core")
    every = gx + ("gy",)

    def passed_x(value, by):
        return lax.ppermute(value, gx, [(i, i + by) for i in range(length_x) if 0 <= i + by < length_x])

    def passed_y(value, by):
        return lax.ppermute(value, "gy", [(i, i + by) for i in range(length_y) if 0 <= i + by < length_y])

    def per_device(orbitals, potential, cell_stiffness):
        node_count, orbital_count = orbitals.shape
        norm_scale = 1.0 / math.sqrt(node_count * length_x * length_y)
        block_rows = orbital_count // length_x
        block_cols = orbital_count // length_y
        half = orbital_count // 2
        quarter = orbital_count // 4
        padded = -(-OWN // 128) * 128

        def by_orbital(rows):
            return (rows, orbital_count)

        def staged(*rows):
            return tuple(pltpu.VMEM(by_orbital(n), F32) for n in rows)

        weight = potential[:, None]
        inside = jnp.stack([lax.axis_index(gx), lax.axis_index("gy")])
        inside = (inside > 0).astype(F32)
        message_rows = 2 * RIM + FACE
        raw_rows = RIM + FACE

        above_x = passed_x(orbitals[:FACE], -1)
        field, ordered, own_columns, partial, message = call(
            prepare,
            (by_orbital(OWN), BF16),
            ((CELL, CELL), F32),
            ((CELL, OWN), BF16),
            (by_orbital(CELL), F32),
            (by_orbital(message_rows), BF16),
            scratch=(
                pltpu.VMEM((SIDE**3, SIDE**3), BF16),
                *staged(OWN, message_rows),
                pltpu.SemaphoreType.DMA((2,)),
            ),
            raw=(0, 1),
        )(orbitals, cell_stiffness)
        message = passed_x(message, 1)
        own_x, rim_x, face_x, own_y, side_y, face_y, edge_y = call(
            split_matrix,
            ((OWN, FACE), BF16),
            ((RIM, FACE), BF16),
            ((FACE, FACE), BF16),
            ((OWN, RIM), BF16),
            ((FACE, RIM), BF16),
            ((FACE, RIM), BF16),
            ((DEG, RIM), BF16),
        )(ordered)

        def row_part(partial, values, above_x, message):
            upward, downward, rim = call(
                cross,
                (by_orbital(FACE), F32),
                (by_orbital(raw_rows), BF16),
                (by_orbital(RIM), F32),
                scratch=staged(message_rows, FACE, raw_rows),
                scalar=(0,),
            )(inside, rim_x, face_x, partial, values, above_x, message)
            from_y = passed_y(upward, 1)
            above_y = passed_y(downward, -1)
            own = call(gather_row, (by_orbital(OWN), F32), scratch=staged(RIM, FACE), scalar=(0,))(
                inside, own_x, face_y, edge_y, partial, values, above_x, rim, downward
            )[0]
            return own, from_y, above_y

        own, from_y, above_y = row_part(partial, field, above_x, message)
        lifted, partial, lowest, message = call(
            lift,
            (by_orbital(OWN), BF16),
            (by_orbital(CELL), F32),
            (by_orbital(FACE), BF16),
            (by_orbital(message_rows), BF16),
            scratch=staged(OWN, RIM, message_rows),
            scalar=(0,),
        )(inside, own_y, side_y, own, from_y, above_y, field, weight, own_columns)
        above_x = passed_x(lowest, -1)
        message = passed_x(message, 1)
        own, from_y, above_y = row_part(partial, lifted, above_x, message)

        def filter_and_gram(
            inside, own_y, side_y, own, from_y, above_y, field, lifted, potential,
            filtered, out, image, far, rows,
        ):
            close(inside, own_y, side_y, own, from_y, above_y, image, far)
            image[OWN:, :] = jnp.zeros((padded - OWN, orbital_count), F32)
            rows[OWN:, :] = jnp.zeros((padded - OWN, orbital_count), F32)
            rows[:OWN, :] = lifted[...].astype(F32)
            lifted32 = rows[:OWN, :]
            image[:OWN, :] += potential[...] * lifted32
            place = lax.broadcasted_iota(jnp.int32, (orbital_count, 1), 0)
            low = lax.bitwise_and(place, quarter - 1)
            line = lax.shift_right_logical(low, block_rows.bit_length() - 1)
            side = lax.shift_right_logical(place, quarter.bit_length() - 1)
            order = (
                line * (4 * block_rows)
                + lax.bitwise_and(side, 1) * (2 * block_rows)
                + lax.shift_right_logical(side, 1) * block_rows
                + lax.bitwise_and(low, block_rows - 1)
            )
            shuffle = one_hot(order, orbital_count)

            def gram(which, left, right):
                shuffled = dot_columns(right, shuffle).astype(BF16)
                product = (dot_rows(left, shuffled) * norm_scale).astype(BF16)
                out[0, which] = product[:, :half]
                out[1, which] = product[:, half:]

            gram(0, image[...].astype(BF16), rows[...].astype(BF16))
            image[:OWN, :] = (
                2.0 * (image[:OWN, :] - SPECTRUM_CENTER * lifted32) / SPECTRUM_HALF - field[...].astype(F32)
            )
            filtered[...] = image[:OWN, :].astype(BF16)
            values = image[...].astype(BF16)
            gram(1, values, values)

        filtered, terms = call(
            filter_and_gram,
            (by_orbital(OWN), BF16),
            ((2, 2, orbital_count, half), BF16),
            scratch=staged(padded, RIM, padded),
            results=(0,),
            scalar=(0,),
        )(inside, own_y, side_y, own, from_y, above_y, field, lifted, weight)

        def pair_sum(terms, out):
            for which in range(2):
                total = (terms[0, which].astype(F32) + terms[1, which].astype(F32)).astype(BF16)
                for side in range(2):
                    part = total[:, side * quarter : (side + 1) * quarter]
                    for j in range(length_y):
                        out[side, j, which * block_cols : (which + 1) * block_cols] = part[
                            j * block_cols : (j + 1) * block_cols
                        ]

        wide = 2 * block_cols
        fold = max(1, 128 // wide)
        short = block_rows // fold

        def plane_sum(terms, out):
            total = terms[0].astype(F32)
            for source in range(1, 2 * length_y):
                total += terms[source].astype(F32)
            total = total.T.reshape(length_z, block_rows, wide)
            for part in range(fold):
                out[:, :, part * wide : (part + 1) * wide] = total[:, part * short : (part + 1) * short, :]

        def line_sum(terms, ham, correlation):
            total = terms[0]
            for source in range(1, length_z):
                total += terms[source]
            for part in range(fold):
                block = total[:, part * wide : (part + 1) * wide]
                ham[part * short : (part + 1) * short, :] = block[:, :block_cols]
                correlation[part * short : (part + 1) * short, :] = block[:, block_cols:]

        terms = lax.all_to_all(terms, "core", 0, 0, tiled=True)
        terms = call(pair_sum, ((2, length_y, wide, quarter), BF16))(terms)[0]
        terms = terms.reshape(2 * length_y, wide, quarter)
        terms = lax.all_to_all(terms, ("half", "gy"), 0, 0, tiled=True)
        terms = call(plane_sum, ((length_z, short, fold * wide), F32))(terms)[0]
        terms = lax.all_to_all(terms, "z", 0, 0, tiled=True)
        block = (block_rows, block_cols)
        projected_ham, correlation = call(line_sum, (block, F32), (block, F32), results=(0, 1))(terms)
        return filtered, projected_ham, correlation

    return jax.shard_map(
        per_device,
        mesh=split_mesh,
        in_specs=(P(every, None), P(every), P()),
        out_specs=(P(every, None), P(gx, "gy"), P(gx, "gy")),
        check_vma=False,
    )
```

```python
import math

import jax
import jax.numpy as jnp
from jax import lax
from jax.experimental import pallas as pl
from jax.experimental.pallas import tpu as pltpu
from jax.sharding import Mesh, PartitionSpec as P

DEG = 7
SIDE = DEG + 1
FACE = DEG * DEG
RIM = FACE + DEG
OWN = FACE * DEG
CELL = OWN + RIM + FACE
SPECTRUM_CENTER = 2.0
SPECTRUM_HALF = 2.0
VMEM_LIMIT = 24 * 2**20
F32 = jnp.float32
BF16 = jnp.bfloat16


def dot(left, right):
    return jnp.dot(left, right, preferred_element_type=F32)


def dot_rows(left, right):
    return lax.dot_general(left, right, (((0,), (0,)), ((), ())), preferred_element_type=F32)


def dot_columns(left, right):
    return lax.dot_general(left, right, (((1,), (1,)), ((), ())), preferred_element_type=F32)


def one_hot(column, width):
    return (column == lax.broadcasted_iota(jnp.int32, (column.shape[0], width), 1)).astype(F32).astype(BF16)


def node_order():
    place = lax.broadcasted_iota(jnp.int32, (CELL, 1), 0)

    def seventh(n):
        return lax.shift_right_logical(n * 9363, 16)

    column = seventh(place)
    plane = seventh(column)
    own = plane * SIDE * SIDE + (column - plane * DEG) * SIDE + (place - column * DEG)
    rim = place - OWN
    rim = DEG * SIDE * SIDE + seventh(rim) * SIDE + (rim - seventh(rim) * DEG)
    face = place - OWN - RIM
    face = seventh(face) * SIDE * SIDE + DEG * SIDE + (face - seventh(face) * DEG)
    return jnp.where(place < OWN, own, jnp.where(place < OWN + RIM, rim, face))


def call(kernel, *shapes, scratch=(), results=(), raw=()):
    def run(*args):
        vmem = pl.BlockSpec(memory_space=pltpu.VMEM)
        places = [
            pl.BlockSpec(memory_space=pl.ANY)
            if i in raw
            else vmem
            for i in range(len(args))
        ]
        return pl.pallas_call(
            kernel,
            out_shape=[
                jax.ShapeDtypeStruct(*shape) if i in results else pltpu.VMEM(*shape) for i, shape in enumerate(shapes)
            ],
            in_specs=places,
            out_specs=[vmem] * len(shapes),
            scratch_shapes=list(scratch),
            compiler_params=pltpu.CompilerParams(vmem_limit_bytes=VMEM_LIMIT),
            name=kernel.__name__,
        )(
            *[
                pltpu.with_memory_space_constraint(arg, pltpu.HBM if i in raw else pltpu.VMEM)
                for i, arg in enumerate(args)
            ]
        )

    return run


def chosen(upper, messages, arrived):
    far, near = messages

    @pl.when(upper)
    def _():
        arrived(near, far)

    @pl.when(jnp.logical_not(upper))
    def _():
        arrived(far, near)


def send(upper, far, near, upward, downward):
    @pl.when(upper)
    def _():
        far[...] = upward[...].astype(BF16)
        near[: downward.shape[0], :] = downward[...].astype(BF16)

    @pl.when(jnp.logical_not(upper))
    def _():
        near[...] = upward[...].astype(BF16)
        far[: downward.shape[0], :] = downward[...].astype(BF16)


def stage_parts(values, stage):
    count = values.shape[0]
    high = values.astype(BF16).astype(F32)
    stage[:count, :] = high
    stage[count : 2 * count, :] = values - high


def stage_plane(values, stage, start):
    for i in range(DEG):
        stage[start + i * DEG : start + (i + 1) * DEG, :] = values[i * FACE : i * FACE + DEG, :]


def pack_x(partial, wide, far, near, upward, downward):
    stage_parts(partial[OWN : OWN + RIM, :], upward)
    stage_plane(wide, upward, 2 * RIM)
    downward[...] = wide[:FACE, :]
    send(lax.axis_index("core") == 1, far, near, upward, downward)


def inside_x():
    return (lax.axis_index("z") + lax.axis_index("half") + lax.axis_index("core") > 0).astype(F32)


def inside_y():
    return (lax.axis_index("gy") > 0).astype(F32)


def prepare(
    field_in, stiffness_in, field, ordered, own_columns, partial, far, near, stiffness, wide, upward, downward, sems
):
    copies = [
        pltpu.make_async_copy(stiffness_in, stiffness, sems.at[0]),
        pltpu.make_async_copy(field_in, field, sems.at[1]),
    ]
    for copy in copies:
        copy.start()
    order = one_hot(node_order(), SIDE**3)
    copies[0].wait()
    ordered[...] = dot_columns(dot(order, stiffness[...]).astype(BF16), order)
    own_columns[...] = ordered[:, :OWN].astype(BF16)
    copies[1].wait()
    partial[...] = dot(own_columns[...], field[...])
    wide[...] = field[...].astype(F32)
    pack_x(partial, wide, far, near, upward, downward)


def split_matrix(ordered, own_x, rim_x, face_x, own_y, side_y, face_y, edge_y):
    to_x, to_y = OWN, OWN + FACE
    own_x[...] = ordered[:OWN, to_x:to_y].astype(BF16)
    rim_x[...] = ordered[OWN : OWN + RIM, to_x:to_y].astype(BF16)
    face_x[...] = ordered[OWN + RIM :, to_x:to_y].astype(BF16)
    own_y[...] = ordered[:OWN, to_y:].astype(BF16)
    side_y[...] = ordered[OWN : OWN + FACE, to_y:].astype(BF16)
    face_y[...] = ordered[OWN + RIM :, to_y:].astype(BF16)
    edge_y[...] = ordered[OWN + FACE : OWN + RIM, to_y:].astype(BF16)


def cross(rim_x, face_x, partial, field, far_in, near_in, far, near, rim, above_x, raw, wide, face, upward, downward):
    def arrived(below, above):
        wide[...] = below[...].astype(F32)
        face[...] = above[:FACE, :].astype(F32)

    chosen(lax.axis_index("core") == 1, (far_in, near_in), arrived)
    above_x[...] = face[...].astype(BF16)
    rim[...] = wide[:RIM, :] + wide[RIM : 2 * RIM, :] + inside_x() * dot(rim_x[...], field[:FACE, :])
    row = partial[OWN + RIM :, :] + dot(face_x[...], above_x[...])
    wide[:FACE, :] = row
    wide[:DEG, :] += rim[FACE:, :]
    upward[...] = jnp.zeros_like(upward)
    stage_parts(wide[:FACE, :], upward)
    downward[:DEG, :] = face[:DEG, :]
    stage_plane(field[...].astype(F32), downward, DEG)
    downward[RIM:, :] = wide[2 * RIM :, :]
    raw[...] = downward[...].astype(BF16)
    send(lax.bitwise_and(lax.axis_index("gy"), 1) == 1, far, near, upward, downward)


def gather_row(own_x, face_y, edge_y, partial, field, above_x, rim, raw, own, corner, face):
    own[...] = partial[:OWN, :] + dot(own_x[...], above_x[...])
    own[:FACE, :] += rim[:FACE, :]
    face[...] = inside_y() * dot(face_y[...], raw[:RIM, :])
    for i in range(DEG):
        own[i * FACE : i * FACE + DEG, :] += face[i * DEG : (i + 1) * DEG, :]
    wide = raw[...].astype(F32)
    corner[:DEG, :] = field[...].astype(F32)[:DEG]
    corner[DEG:, :] = wide[RIM:]
    own[:DEG, :] += inside_x() * inside_y() * dot(edge_y[...], corner[...].astype(BF16))


def close(own_y, side_y, own, far_in, near_in, image, corner, face, wide):
    def arrived(below, above):
        parts = below[...].astype(F32)
        face[...] = parts[:FACE, :] + parts[FACE : 2 * FACE, :]
        wide[...] = above[...].astype(F32)

    chosen(lax.bitwise_and(lax.axis_index("gy"), 1) == 1, (far_in, near_in), arrived)
    corner[:DEG, :] = wide[DEG : 2 * DEG, :]
    corner[DEG:, :] = wide[RIM:, :]
    image[:OWN, :] = own[...] + dot(own_y[...], wide[:RIM, :].astype(BF16))
    image[:FACE, :] += inside_x() * dot(side_y[...], corner[...].astype(BF16))
    for i in range(DEG):
        image[i * FACE : i * FACE + DEG, :] += face[i * DEG : (i + 1) * DEG, :]


def lift(
    own_y, side_y, own, far_in, near_in, field, potential, own_columns,
    lifted, partial, far, near, image, corner, face, wide, upward,
):
    close(own_y, side_y, own, far_in, near_in, image, corner, face, wide)
    field32 = field[...].astype(F32)
    first_image = image[...] + potential[...] * field32
    image[...] = (first_image - SPECTRUM_CENTER * field32) / SPECTRUM_HALF
    lifted[...] = image[...].astype(BF16)
    partial[...] = dot(own_columns[...], lifted[...])
    pack_x(partial, image, far, near, upward, face)


def solution(mesh):
    length_x, length_y = mesh.shape["gx"], mesh.shape["gy"]
    length_z = length_x // 4
    split_mesh = Mesh(mesh.devices.reshape(length_z, 2, 2, length_y), ("z", "half", "core", "gy"))
    gx = ("z", "half", "core")
    every = gx + ("gy",)

    def swapped(far, near, axis, length):
        def pairs(first):
            return [(i + j, i + 1 - j) for i in range(first, length - 1, 2) for j in range(2)]

        return lax.ppermute(far, axis, pairs(1)), lax.ppermute(near, axis, pairs(0))

    def per_device(orbitals, potential, cell_stiffness):
        node_count, orbital_count = orbitals.shape
        norm_scale = 1.0 / math.sqrt(node_count * length_x * length_y)
        block_rows = orbital_count // length_x
        block_cols = orbital_count // length_y
        half = orbital_count // 2
        quarter = orbital_count // 4
        padded = -(-OWN // 128) * 128

        def by_orbital(rows):
            return (rows, orbital_count)

        def staged(*rows):
            return tuple(pltpu.VMEM(by_orbital(n), F32) for n in rows)

        weight = potential[:, None]
        message_rows = 2 * RIM + FACE
        raw_rows = RIM + FACE

        field, ordered, own_columns, partial, far, near = call(
            prepare,
            (by_orbital(OWN), BF16),
            ((CELL, CELL), F32),
            ((CELL, OWN), BF16),
            (by_orbital(CELL), F32),
            (by_orbital(message_rows), BF16),
            (by_orbital(message_rows), BF16),
            scratch=(
                pltpu.VMEM((SIDE**3, SIDE**3), BF16),
                *staged(OWN, message_rows, FACE),
                pltpu.SemaphoreType.DMA((2,)),
            ),
            raw=(0, 1),
        )(orbitals, cell_stiffness)
        far, near = swapped(far, near, gx, length_x)
        own_x, rim_x, face_x, own_y, side_y, face_y, edge_y = call(
            split_matrix,
            ((OWN, FACE), BF16),
            ((RIM, FACE), BF16),
            ((FACE, FACE), BF16),
            ((OWN, RIM), BF16),
            ((FACE, RIM), BF16),
            ((FACE, RIM), BF16),
            ((DEG, RIM), BF16),
        )(ordered)

        def row_part(partial, values, far, near):
            far, near, rim, above_x, raw = call(
                cross,
                (by_orbital(raw_rows), BF16),
                (by_orbital(raw_rows), BF16),
                (by_orbital(RIM), F32),
                (by_orbital(FACE), BF16),
                (by_orbital(raw_rows), BF16),
                scratch=staged(message_rows, FACE, raw_rows, raw_rows),
            )(rim_x, face_x, partial, values, far, near)
            far, near = swapped(far, near, "gy", length_y)
            own = call(gather_row, (by_orbital(OWN), F32), scratch=staged(RIM, FACE))(
                own_x, face_y, edge_y, partial, values, above_x, rim, raw
            )[0]
            return own, far, near

        own, far, near = row_part(partial, field, far, near)
        lifted, partial, far, near = call(
            lift,
            (by_orbital(OWN), BF16),
            (by_orbital(CELL), F32),
            (by_orbital(message_rows), BF16),
            (by_orbital(message_rows), BF16),
            scratch=staged(OWN, RIM, FACE, raw_rows, message_rows),
        )(own_y, side_y, own, far, near, field, weight, own_columns)
        far, near = swapped(far, near, gx, length_x)
        own, far, near = row_part(partial, lifted, far, near)

        def filter_and_gram(
            own_y, side_y, own, far_in, near_in, field, lifted, potential,
            filtered, out, image, corner, face, wide, rows,
        ):
            close(own_y, side_y, own, far_in, near_in, image, corner, face, wide)
            image[OWN:, :] = jnp.zeros((padded - OWN, orbital_count), F32)
            rows[OWN:, :] = jnp.zeros((padded - OWN, orbital_count), F32)
            rows[:OWN, :] = lifted[...].astype(F32)
            lifted32 = rows[:OWN, :]
            image[:OWN, :] += potential[...] * lifted32
            place = lax.broadcasted_iota(jnp.int32, (orbital_count, 1), 0)
            low = lax.bitwise_and(place, quarter - 1)
            line = lax.shift_right_logical(low, block_rows.bit_length() - 1)
            side = lax.shift_right_logical(place, quarter.bit_length() - 1)
            order = (
                line * (4 * block_rows)
                + lax.bitwise_and(side, 1) * (2 * block_rows)
                + lax.shift_right_logical(side, 1) * block_rows
                + lax.bitwise_and(low, block_rows - 1)
            )
            shuffle = one_hot(order, orbital_count)

            def gram(which, left, right):
                shuffled = dot_columns(right, shuffle).astype(BF16)
                product = (dot_rows(left, shuffled) * norm_scale).astype(BF16)
                out[0, which] = product[:, :half]
                out[1, which] = product[:, half:]

            gram(0, image[...].astype(BF16), rows[...].astype(BF16))
            image[:OWN, :] = (
                2.0 * (image[:OWN, :] - SPECTRUM_CENTER * lifted32) / SPECTRUM_HALF - field[...].astype(F32)
            )
            filtered[...] = image[:OWN, :].astype(BF16)
            values = image[...].astype(BF16)
            gram(1, values, values)

        filtered, terms = call(
            filter_and_gram,
            (by_orbital(OWN), BF16),
            ((2, 2, orbital_count, half), BF16),
            scratch=staged(padded, RIM, FACE, raw_rows, padded),
            results=(0,),
        )(own_y, side_y, own, far, near, field, lifted, weight)

        def pair_sum(terms, out):
            for which in range(2):
                total = (terms[0, which].astype(F32) + terms[1, which].astype(F32)).astype(BF16)
                for side in range(2):
                    part = total[:, side * quarter : (side + 1) * quarter]
                    for j in range(length_y):
                        out[side, j, which * block_cols : (which + 1) * block_cols] = part[
                            j * block_cols : (j + 1) * block_cols
                        ]

        wide = 2 * block_cols
        fold = max(1, 128 // wide)
        short = block_rows // fold

        def plane_sum(terms, out):
            total = terms[0].astype(F32)
            for source in range(1, 2 * length_y):
                total += terms[source].astype(F32)
            total = total.T.reshape(length_z, block_rows, wide)
            for part in range(fold):
                out[:, :, part * wide : (part + 1) * wide] = total[:, part * short : (part + 1) * short, :]

        def line_sum(terms, ham, correlation):
            total = terms[0]
            for source in range(1, length_z):
                total += terms[source]
            for part in range(fold):
                block = total[:, part * wide : (part + 1) * wide]
                ham[part * short : (part + 1) * short, :] = block[:, :block_cols]
                correlation[part * short : (part + 1) * short, :] = block[:, block_cols:]

        terms = lax.all_to_all(terms, "core", 0, 0, tiled=True)
        terms = call(pair_sum, ((2, length_y, wide, quarter), BF16))(terms)[0]
        terms = terms.reshape(2 * length_y, wide, quarter)
        terms = lax.all_to_all(terms, ("half", "gy"), 0, 0, tiled=True)
        terms = call(plane_sum, ((length_z, short, fold * wide), F32))(terms)[0]
        terms = lax.all_to_all(terms, "z", 0, 0, tiled=True)
        block = (block_rows, block_cols)
        projected_ham, correlation = call(line_sum, (block, F32), (block, F32), results=(0, 1))(terms)
        return filtered, projected_ham, correlation

    return jax.shard_map(
        per_device,
        mesh=split_mesh,
        in_specs=(P(every, None), P(every), P()),
        out_specs=(P(every, None), P(gx, "gy"), P(gx, "gy")),
        check_vma=False,
    )
```

```python
import math

import jax
import jax.numpy as jnp
from jax import lax
from jax.experimental import pallas as pl
from jax.experimental.pallas import tpu as pltpu
from jax.sharding import Mesh, PartitionSpec as P


DEG = 7
SIDE = DEG + 1
FACE = DEG * DEG
RIM = FACE + DEG
OWN = FACE * DEG
CELL = OWN + RIM + FACE
SPECTRUM_CENTER = 2.0
SPECTRUM_HALF = 2.0
VMEM_LIMIT = 24 * 2**20
F32 = jnp.float32
BF16 = jnp.bfloat16


def dot(left, right):
    return jnp.dot(left, right, preferred_element_type=F32)


def dot_rows(left, right):
    return lax.dot_general(left, right, (((0,), (0,)), ((), ())), preferred_element_type=F32)


def dot_columns(left, right):
    return lax.dot_general(left, right, (((1,), (1,)), ((), ())), preferred_element_type=F32)


def one_hot(column, width):
    return (column == lax.broadcasted_iota(jnp.int32, (column.shape[0], width), 1)).astype(F32).astype(BF16)


def node_order(first, count):
    place = first + lax.broadcasted_iota(jnp.int32, (count, 1), 0)

    def seventh(n):
        return lax.shift_right_logical(n * 9363, 16)

    column = seventh(place)
    plane = seventh(column)
    own = plane * SIDE * SIDE + (column - plane * DEG) * SIDE + (place - column * DEG)
    rim = place - OWN
    rim = DEG * SIDE * SIDE + seventh(rim) * SIDE + (rim - seventh(rim) * DEG)
    face = place - OWN - RIM
    face = seventh(face) * SIDE * SIDE + DEG * SIDE + (face - seventh(face) * DEG)
    return jnp.where(place < OWN, own, jnp.where(place < OWN + RIM, rim, face))


def call(kernel, *shapes, scratch=(), results=(), raw=()):
    def run(*args):
        vmem = pl.BlockSpec(memory_space=pltpu.VMEM)
        places = [
            pl.BlockSpec(memory_space=pl.ANY)
            if i in raw
            else vmem
            for i in range(len(args))
        ]
        return pl.pallas_call(
            kernel,
            out_shape=[
                jax.ShapeDtypeStruct(*shape) if i in results else pltpu.VMEM(*shape) for i, shape in enumerate(shapes)
            ],
            in_specs=places,
            out_specs=[vmem] * len(shapes),
            scratch_shapes=list(scratch),
            compiler_params=pltpu.CompilerParams(vmem_limit_bytes=VMEM_LIMIT),
        )(
            *[
                pltpu.with_memory_space_constraint(arg, pltpu.HBM if i in raw else pltpu.VMEM)
                for i, arg in enumerate(args)
            ]
        )

    return run


def chosen(upper, messages, arrived):
    far, near = messages

    @pl.when(upper)
    def _():
        arrived(near, far)

    @pl.when(jnp.logical_not(upper))
    def _():
        arrived(far, near)


def send(upper, far, near, upward, downward):
    @pl.when(upper)
    def _():
        far[...] = upward[...].astype(BF16)
        near[: downward.shape[0], :] = downward[...].astype(BF16)

    @pl.when(jnp.logical_not(upper))
    def _():
        near[...] = upward[...].astype(BF16)
        far[: downward.shape[0], :] = downward[...].astype(BF16)


def stage_parts(values, stage):
    count = values.shape[0]
    high = values.astype(BF16).astype(F32)
    stage[:count, :] = high
    stage[count : 2 * count, :] = values - high


def stage_plane(values, stage, start):
    for i in range(DEG):
        stage[start + i * DEG : start + (i + 1) * DEG, :] = values[i * FACE : i * FACE + DEG, :]


def pack_x(rim, wide, far, near, upward, downward):
    upward[:RIM, :] = rim
    stage_plane(wide, upward, RIM)
    downward[...] = wide[:FACE, :]
    send(lax.axis_index("core") == 1, far, near, upward, downward)


def inside_x():
    return (lax.axis_index("z") + lax.axis_index("half") + lax.axis_index("core") > 0).astype(F32)


def inside_y():
    return (lax.axis_index("gy") > 0).astype(F32)


def prepare(field_in, stiffness_in, field, stiffness, rim_own, far, near, wide, upward, downward, sems):
    copies = [
        pltpu.make_async_copy(stiffness_in, stiffness, sems.at[0]),
        pltpu.make_async_copy(field_in, field, sems.at[1]),
    ]
    for copy in copies:
        copy.start()
    nodes = one_hot(node_order(0, OWN), SIDE**3)
    rim = one_hot(node_order(OWN, RIM), SIDE**3)
    copies[0].wait()
    rim_own[...] = dot_columns(dot(rim, stiffness[...]).astype(BF16), nodes).astype(BF16)
    copies[1].wait()
    wide[...] = field[...].astype(F32)
    pack_x(dot(rim_own[...], field[...]), wide, far, near, upward, downward)


def arrange(stiffness, field, own_columns, partial, own_x, rim_x, face_x, own_y, side_y, face_y, edge_y, ordered):
    order = one_hot(node_order(0, CELL), SIDE**3)
    ordered[...] = dot_columns(dot(order, stiffness[...]).astype(BF16), order)
    own_columns[...] = ordered[:, :OWN].astype(BF16)
    partial[...] = dot(own_columns[...], field[...])
    to_x, to_y = OWN, OWN + FACE
    own_x[...] = ordered[:OWN, to_x:to_y].astype(BF16)
    rim_x[...] = ordered[OWN : OWN + RIM, to_x:to_y].astype(BF16)
    face_x[...] = ordered[OWN + RIM :, to_x:to_y].astype(BF16)
    own_y[...] = ordered[:OWN, to_y:].astype(BF16)
    side_y[...] = ordered[OWN : OWN + FACE, to_y:].astype(BF16)
    face_y[...] = ordered[OWN + RIM :, to_y:].astype(BF16)
    edge_y[...] = ordered[OWN + FACE : OWN + RIM, to_y:].astype(BF16)


def multiply(own_columns, field, partial):
    partial[...] = dot(own_columns[...], field[...])


def cross(rim_x, face_x, partial, field, far_in, near_in, far, near, rim, above_x, raw, wide, face, upward, downward):
    def arrived(below, above):
        wide[...] = below[...].astype(F32)
        face[...] = above[:FACE, :].astype(F32)

    chosen(lax.axis_index("core") == 1, (far_in, near_in), arrived)
    above_x[...] = face[...].astype(BF16)
    rim[...] = wide[:RIM, :] + inside_x() * dot(rim_x[...], field[:FACE, :])
    row = partial[OWN + RIM :, :] + dot(face_x[...], above_x[...])
    downward[:DEG, :] = face[:DEG, :]
    stage_plane(field[...].astype(F32), downward, DEG)
    downward[RIM:, :] = wide[RIM:, :]
    wide[:FACE, :] = row
    wide[:DEG, :] += rim[FACE:, :]
    upward[...] = jnp.zeros_like(upward)
    stage_parts(wide[:FACE, :], upward)
    raw[...] = downward[...].astype(BF16)
    send(lax.bitwise_and(lax.axis_index("gy"), 1) == 1, far, near, upward, downward)


def gather_row(own_x, face_y, edge_y, partial, field, above_x, rim, raw, own, corner, face):
    own[...] = partial[:OWN, :] + dot(own_x[...], above_x[...])
    own[:FACE, :] += rim[:FACE, :]
    face[...] = inside_y() * dot(face_y[...], raw[:RIM, :])
    for i in range(DEG):
        own[i * FACE : i * FACE + DEG, :] += face[i * DEG : (i + 1) * DEG, :]
    wide = raw[...].astype(F32)
    corner[:DEG, :] = field[...].astype(F32)[:DEG]
    corner[DEG:, :] = wide[RIM:]
    own[:DEG, :] += inside_x() * inside_y() * dot(edge_y[...], corner[...].astype(BF16))


def close(own_y, side_y, own, far_in, near_in, image, corner, face, wide):
    def arrived(below, above):
        parts = below[...].astype(F32)
        face[...] = parts[:FACE, :] + parts[FACE : 2 * FACE, :]
        wide[...] = above[...].astype(F32)

    chosen(lax.bitwise_and(lax.axis_index("gy"), 1) == 1, (far_in, near_in), arrived)
    corner[:DEG, :] = wide[DEG : 2 * DEG, :]
    corner[DEG:, :] = wide[RIM:, :]
    image[:OWN, :] = own[...] + dot(own_y[...], wide[:RIM, :].astype(BF16))
    image[:FACE, :] += inside_x() * dot(side_y[...], corner[...].astype(BF16))
    for i in range(DEG):
        image[i * FACE : i * FACE + DEG, :] += face[i * DEG : (i + 1) * DEG, :]


def lift(
    own_y, side_y, own, far_in, near_in, field, potential, rim_own,
    lifted, far, near, image, corner, face, wide, upward,
):
    close(own_y, side_y, own, far_in, near_in, image, corner, face, wide)
    field32 = field[...].astype(F32)
    first_image = image[...] + potential[...] * field32
    image[...] = (first_image - SPECTRUM_CENTER * field32) / SPECTRUM_HALF
    lifted[...] = image[...].astype(BF16)
    pack_x(dot(rim_own[...], lifted[...]), image, far, near, upward, face)


def solution(mesh):
    length_x, length_y = mesh.shape["gx"], mesh.shape["gy"]
    length_z = length_x // 4
    split_mesh = Mesh(mesh.devices.reshape(length_z, 2, 2, length_y), ("z", "half", "core", "gy"))
    gx = ("z", "half", "core")
    every = gx + ("gy",)

    def swapped(far, near, axis, length):
        def pairs(first):
            return [(i + j, i + 1 - j) for i in range(first, length - 1, 2) for j in range(2)]

        return lax.ppermute(far, axis, pairs(1)), lax.ppermute(near, axis, pairs(0))

    def per_device(orbitals, potential, cell_stiffness):
        node_count, orbital_count = orbitals.shape
        norm_scale = 1.0 / math.sqrt(node_count * length_x * length_y)
        block_rows = orbital_count // length_x
        block_cols = orbital_count // length_y
        half = orbital_count // 2
        quarter = orbital_count // 4
        padded = -(-OWN // 128) * 128

        def by_orbital(rows):
            return (rows, orbital_count)

        def staged(*rows):
            return tuple(pltpu.VMEM(by_orbital(n), F32) for n in rows)

        weight = potential[:, None]
        message_rows = RIM + FACE
        message = (by_orbital(message_rows), BF16)

        field, stiffness, rim_own, far, near = call(
            prepare,
            (by_orbital(OWN), BF16),
            ((SIDE**3, SIDE**3), BF16),
            ((RIM, OWN), BF16),
            message,
            message,
            scratch=(*staged(OWN, message_rows, FACE), pltpu.SemaphoreType.DMA((2,))),
            raw=(0, 1),
        )(orbitals, cell_stiffness)
        far, near = swapped(far, near, gx, length_x)
        own_columns, partial, own_x, rim_x, face_x, own_y, side_y, face_y, edge_y = call(
            arrange,
            ((CELL, OWN), BF16),
            (by_orbital(CELL), F32),
            ((OWN, FACE), BF16),
            ((RIM, FACE), BF16),
            ((FACE, FACE), BF16),
            ((OWN, RIM), BF16),
            ((FACE, RIM), BF16),
            ((FACE, RIM), BF16),
            ((DEG, RIM), BF16),
            scratch=(pltpu.VMEM((CELL, CELL), F32),),
        )(stiffness, field)

        def row_part(partial, values, far, near):
            far, near, rim, above_x, raw = call(
                cross,
                message,
                message,
                (by_orbital(RIM), F32),
                (by_orbital(FACE), BF16),
                message,
                scratch=staged(message_rows, FACE, message_rows, message_rows),
            )(rim_x, face_x, partial, values, far, near)
            far, near = swapped(far, near, "gy", length_y)
            own = call(gather_row, (by_orbital(OWN), F32), scratch=staged(RIM, FACE))(
                own_x, face_y, edge_y, partial, values, above_x, rim, raw
            )[0]
            return own, far, near

        own, far, near = row_part(partial, field, far, near)
        lifted, far, near = call(
            lift,
            (by_orbital(OWN), BF16),
            message,
            message,
            scratch=staged(OWN, RIM, FACE, message_rows, message_rows),
        )(own_y, side_y, own, far, near, field, weight, rim_own)
        far, near = swapped(far, near, gx, length_x)
        partial = call(multiply, (by_orbital(CELL), F32))(own_columns, lifted)[0]
        own, far, near = row_part(partial, lifted, far, near)

        def shuffle():
            place = lax.broadcasted_iota(jnp.int32, (orbital_count, 1), 0)
            low = lax.bitwise_and(place, quarter - 1)
            line = lax.shift_right_logical(low, block_rows.bit_length() - 1)
            side = lax.shift_right_logical(place, quarter.bit_length() - 1)
            order = (
                line * (4 * block_rows)
                + lax.bitwise_and(side, 1) * (2 * block_rows)
                + lax.shift_right_logical(side, 1) * block_rows
                + lax.bitwise_and(low, block_rows - 1)
            )
            return one_hot(order, orbital_count)

        def gram(left, right, keep, give):
            shuffled = dot_columns(right, shuffle()).astype(BF16)
            product = (dot_rows(left, shuffled) * norm_scale).astype(BF16)
            core = lax.axis_index("core")

            @pl.when(core == 0)
            def _():
                keep[...] = product[:, :half]
                give[...] = product[:, half:]

            @pl.when(core == 1)
            def _():
                keep[...] = product[:, half:]
                give[...] = product[:, :half]

        def image_gram(
            own_y, side_y, own, far_in, near_in, lifted, potential,
            second_image, keep, give, image, corner, face, wide, rows,
        ):
            close(own_y, side_y, own, far_in, near_in, image, corner, face, wide)
            image[OWN:, :] = jnp.zeros((padded - OWN, orbital_count), F32)
            rows[OWN:, :] = jnp.zeros((padded - OWN, orbital_count), F32)
            rows[:OWN, :] = lifted[...].astype(F32)
            image[:OWN, :] += potential[...] * rows[:OWN, :]
            second_image[...] = image[:OWN, :]
            gram(image[...].astype(BF16), rows[...].astype(BF16), keep, give)

        def filter_gram(second_image, field, lifted, filtered, keep, give, rows):
            rows[OWN:, :] = jnp.zeros((padded - OWN, orbital_count), F32)
            rows[:OWN, :] = (
                2.0 * (second_image[...] - SPECTRUM_CENTER * lifted[...].astype(F32)) / SPECTRUM_HALF
                - field[...].astype(F32)
            )
            filtered[...] = rows[:OWN, :].astype(BF16)
            values = rows[...].astype(BF16)
            gram(values, values, keep, give)

        half_gram = ((orbital_count, half), BF16)
        pair = [(0, 1), (1, 0)]
        second_image, ham_kept, ham_given = call(
            image_gram,
            (by_orbital(OWN), F32),
            half_gram,
            half_gram,
            scratch=staged(padded, RIM, FACE, message_rows, padded),
        )(own_y, side_y, own, far, near, lifted, weight)
        ham_taken = lax.ppermute(ham_given, "core", pair)
        filtered, kept, given = call(
            filter_gram,
            (by_orbital(OWN), BF16),
            half_gram,
            half_gram,
            scratch=staged(padded),
            results=(0,),
        )(second_image, field, lifted)
        taken = lax.ppermute(given, "core", pair)

        def pair_sum(ham_kept, ham_taken, kept, taken, out):
            for which, (mine, other) in enumerate(((ham_kept, ham_taken), (kept, taken))):
                total = (mine[...].astype(F32) + other[...].astype(F32)).astype(BF16)
                for side in range(2):
                    part = total[:, side * quarter : (side + 1) * quarter]
                    for j in range(length_y):
                        out[side, j, which * block_cols : (which + 1) * block_cols] = part[
                            j * block_cols : (j + 1) * block_cols
                        ]

        wide = 2 * block_cols
        fold = max(1, 128 // wide)
        short = block_rows // fold

        def plane_sum(terms, out):
            total = terms[0].astype(F32)
            for source in range(1, 2 * length_y):
                total += terms[source].astype(F32)
            total = total.T.reshape(length_z, block_rows, wide)
            for part in range(fold):
                out[:, :, part * wide : (part + 1) * wide] = total[:, part * short : (part + 1) * short, :]

        def line_sum(terms, ham, correlation):
            total = terms[0]
            for source in range(1, length_z):
                total += terms[source]
            for part in range(fold):
                block = total[:, part * wide : (part + 1) * wide]
                ham[part * short : (part + 1) * short, :] = block[:, :block_cols]
                correlation[part * short : (part + 1) * short, :] = block[:, block_cols:]

        terms = call(pair_sum, ((2, length_y, wide, quarter), BF16))(ham_kept, ham_taken, kept, taken)[0]
        terms = terms.reshape(2 * length_y, wide, quarter)
        terms = lax.all_to_all(terms, ("half", "gy"), 0, 0, tiled=True)
        terms = call(plane_sum, ((length_z, short, fold * wide), F32))(terms)[0]
        terms = lax.all_to_all(terms, "z", 0, 0, tiled=True)
        block = (block_rows, block_cols)
        projected_ham, correlation = call(line_sum, (block, F32), (block, F32), results=(0, 1))(terms)
        return filtered, projected_ham, correlation

    return jax.shard_map(
        per_device,
        mesh=split_mesh,
        in_specs=(P(every, None), P(every), P()),
        out_specs=(P(every, None), P(gx, "gy"), P(gx, "gy")),
        check_vma=False,
    )
```

```python
import math

import jax
import jax.numpy as jnp
from jax import lax
from jax.experimental import pallas as pl
from jax.experimental.pallas import tpu as pltpu
from jax.sharding import Mesh, PartitionSpec as P

DEG = 7
SIDE = DEG + 1
FACE = DEG * DEG
RIM = FACE + DEG
OWN = FACE * DEG
CELL = OWN + RIM + FACE
SPECTRUM_CENTER = 2.0
SPECTRUM_HALF = 2.0
VMEM_LIMIT = 24 * 2**20
F32 = jnp.float32
BF16 = jnp.bfloat16


def dot(left, right):
    return jnp.dot(left, right, preferred_element_type=F32)


def dot_rows(left, right):
    return lax.dot_general(left, right, (((0,), (0,)), ((), ())), preferred_element_type=F32)


def dot_columns(left, right):
    return lax.dot_general(left, right, (((1,), (1,)), ((), ())), preferred_element_type=F32)


def one_hot(column, width):
    return (column == lax.broadcasted_iota(jnp.int32, (column.shape[0], width), 1)).astype(F32).astype(BF16)


def node_order(first, count):
    place = first + lax.broadcasted_iota(jnp.int32, (count, 1), 0)

    def seventh(n):
        return lax.shift_right_logical(n * 9363, 16)

    column = seventh(place)
    plane = seventh(column)
    own = plane * SIDE * SIDE + (column - plane * DEG) * SIDE + (place - column * DEG)
    rim = place - OWN
    rim = DEG * SIDE * SIDE + seventh(rim) * SIDE + (rim - seventh(rim) * DEG)
    face = place - OWN - RIM
    face = seventh(face) * SIDE * SIDE + DEG * SIDE + (face - seventh(face) * DEG)
    return jnp.where(place < OWN, own, jnp.where(place < OWN + RIM, rim, face))


def call(kernel, *shapes, scratch=(), results=(), raw=()):
    def run(*args):
        vmem = pl.BlockSpec(memory_space=pltpu.VMEM)
        places = [
            pl.BlockSpec(memory_space=pl.ANY)
            if i in raw
            else vmem
            for i in range(len(args))
        ]
        return pl.pallas_call(
            kernel,
            out_shape=[
                jax.ShapeDtypeStruct(*shape) if i in results else pltpu.VMEM(*shape) for i, shape in enumerate(shapes)
            ],
            in_specs=places,
            out_specs=[vmem] * len(shapes),
            scratch_shapes=list(scratch),
            compiler_params=pltpu.CompilerParams(vmem_limit_bytes=VMEM_LIMIT),
            name=kernel.__name__,
        )(
            *[
                pltpu.with_memory_space_constraint(arg, pltpu.HBM if i in raw else pltpu.VMEM)
                for i, arg in enumerate(args)
            ]
        )

    return run


def chosen(upper, messages, arrived):
    far, near = messages

    @pl.when(upper)
    def _():
        arrived(near, far)

    @pl.when(jnp.logical_not(upper))
    def _():
        arrived(far, near)


def send(upper, far, near, upward, downward):
    @pl.when(upper)
    def _():
        far[...] = upward[...].astype(BF16)
        near[: downward.shape[0], :] = downward[...].astype(BF16)

    @pl.when(jnp.logical_not(upper))
    def _():
        near[...] = upward[...].astype(BF16)
        far[: downward.shape[0], :] = downward[...].astype(BF16)


def stage_parts(values, stage):
    count = values.shape[0]
    high = values.astype(BF16).astype(F32)
    stage[:count, :] = high
    stage[count : 2 * count, :] = values - high


def stage_plane(values, stage, start):
    for i in range(DEG):
        stage[start + i * DEG : start + (i + 1) * DEG, :] = values[i * FACE : i * FACE + DEG, :]


def pack_x(rim, wide, far, near, upward, downward):
    upward[:RIM, :] = rim
    stage_plane(wide, upward, RIM)
    downward[...] = wide[:FACE, :]
    send(lax.axis_index("core") == 1, far, near, upward, downward)


def inside_x():
    return (lax.axis_index("z") + lax.axis_index("half") + lax.axis_index("core") > 0).astype(F32)


def inside_y():
    return (lax.axis_index("gy") > 0).astype(F32)


def prepare(field_in, stiffness_in, field, stiffness, rim_own, far, near, wide, upward, downward, sems):
    copies = [
        pltpu.make_async_copy(stiffness_in, stiffness, sems.at[0]),
        pltpu.make_async_copy(field_in, field, sems.at[1]),
    ]
    for copy in copies:
        copy.start()
    nodes = one_hot(node_order(0, OWN), SIDE**3)
    rim = one_hot(node_order(OWN, RIM), SIDE**3)
    copies[0].wait()
    rim_own[...] = dot_columns(dot(rim, stiffness[...]).astype(BF16), nodes).astype(BF16)
    copies[1].wait()
    wide[...] = field[...].astype(F32)
    pack_x(dot(rim_own[...], field[...]), wide, far, near, upward, downward)


def arrange(stiffness, field, own_columns, partial, own_x, rim_x, face_x, own_y, side_y, face_y, edge_y, ordered):
    order = one_hot(node_order(0, CELL), SIDE**3)
    ordered[...] = dot_columns(dot(order, stiffness[...]).astype(BF16), order)
    own_columns[...] = ordered[:, :OWN].astype(BF16)
    partial[...] = dot(own_columns[...], field[...])
    to_x, to_y = OWN, OWN + FACE
    own_x[...] = ordered[:OWN, to_x:to_y].astype(BF16)
    rim_x[...] = ordered[OWN : OWN + RIM, to_x:to_y].astype(BF16)
    face_x[...] = ordered[OWN + RIM :, to_x:to_y].astype(BF16)
    own_y[...] = ordered[:OWN, to_y:].astype(BF16)
    side_y[...] = ordered[OWN : OWN + FACE, to_y:].astype(BF16)
    face_y[...] = ordered[OWN + RIM :, to_y:].astype(BF16)
    edge_y[...] = ordered[OWN + FACE : OWN + RIM, to_y:].astype(BF16)


def cross(rim_x, face_x, partial, field, far_in, near_in, far, near, rim, above_x, raw, wide, face, upward, downward):
    def arrived(below, above):
        wide[...] = below[...].astype(F32)
        face[...] = above[:FACE, :].astype(F32)

    chosen(lax.axis_index("core") == 1, (far_in, near_in), arrived)
    above_x[...] = face[...].astype(BF16)
    rim[...] = wide[:RIM, :] + inside_x() * dot(rim_x[...], field[:FACE, :])
    row = partial[OWN + RIM :, :] + dot(face_x[...], above_x[...])
    downward[:DEG, :] = face[:DEG, :]
    stage_plane(field[...].astype(F32), downward, DEG)
    downward[RIM:, :] = wide[RIM:, :]
    wide[:FACE, :] = row
    wide[:DEG, :] += rim[FACE:, :]
    upward[...] = jnp.zeros_like(upward)
    stage_parts(wide[:FACE, :], upward)
    raw[...] = downward[...].astype(BF16)
    send(lax.bitwise_and(lax.axis_index("gy"), 1) == 1, far, near, upward, downward)


def gather_row(own_x, face_y, edge_y, partial, field, above_x, rim, raw, own, corner, face):
    own[...] = partial[:OWN, :] + dot(own_x[...], above_x[...])
    own[:FACE, :] += rim[:FACE, :]
    face[...] = inside_y() * dot(face_y[...], raw[:RIM, :])
    for i in range(DEG):
        own[i * FACE : i * FACE + DEG, :] += face[i * DEG : (i + 1) * DEG, :]
    wide = raw[...].astype(F32)
    corner[:DEG, :] = field[...].astype(F32)[:DEG]
    corner[DEG:, :] = wide[RIM:]
    own[:DEG, :] += inside_x() * inside_y() * dot(edge_y[...], corner[...].astype(BF16))


def close(own_y, side_y, own, far_in, near_in, image, corner, face, wide):
    def arrived(below, above):
        parts = below[...].astype(F32)
        face[...] = parts[:FACE, :] + parts[FACE : 2 * FACE, :]
        wide[...] = above[...].astype(F32)

    chosen(lax.bitwise_and(lax.axis_index("gy"), 1) == 1, (far_in, near_in), arrived)
    corner[:DEG, :] = wide[DEG : 2 * DEG, :]
    corner[DEG:, :] = wide[RIM:, :]
    image[:OWN, :] = own[...] + dot(own_y[...], wide[:RIM, :].astype(BF16))
    image[:FACE, :] += inside_x() * dot(side_y[...], corner[...].astype(BF16))
    for i in range(DEG):
        image[i * FACE : i * FACE + DEG, :] += face[i * DEG : (i + 1) * DEG, :]


def lift(
    own_y, side_y, own, far_in, near_in, field, potential, rim_own,
    lifted, far, near, image, corner, face, wide, upward,
):
    close(own_y, side_y, own, far_in, near_in, image, corner, face, wide)
    field32 = field[...].astype(F32)
    first_image = image[...] + potential[...] * field32
    image[...] = (first_image - SPECTRUM_CENTER * field32) / SPECTRUM_HALF
    lifted[...] = image[...].astype(BF16)
    pack_x(dot(rim_own[...], lifted[...]), image, far, near, upward, face)


def solution(mesh):
    length_x, length_y = mesh.shape["gx"], mesh.shape["gy"]
    length_z = length_x // 4
    split_mesh = Mesh(mesh.devices.reshape(length_z, 2, 2, length_y), ("z", "half", "core", "gy"))
    gx = ("z", "half", "core")
    every = gx + ("gy",)

    def swapped(far, near, axis, length):
        def pairs(first):
            return [(i + j, i + 1 - j) for i in range(first, length - 1, 2) for j in range(2)]

        return lax.ppermute(far, axis, pairs(1)), lax.ppermute(near, axis, pairs(0))

    def per_device(orbitals, potential, cell_stiffness):
        node_count, orbital_count = orbitals.shape
        norm_scale = 1.0 / math.sqrt(node_count * length_x * length_y)
        block_rows = orbital_count // length_x
        block_cols = orbital_count // length_y
        half = orbital_count // 2
        quarter = orbital_count // 4
        padded = -(-OWN // 128) * 128

        def by_orbital(rows):
            return (rows, orbital_count)

        def staged(*rows):
            return tuple(pltpu.VMEM(by_orbital(n), F32) for n in rows)

        weight = potential[:, None]
        message_rows = RIM + FACE
        message = (by_orbital(message_rows), BF16)

        field, stiffness, rim_own, far, near = call(
            prepare,
            (by_orbital(OWN), BF16),
            ((SIDE**3, SIDE**3), BF16),
            ((RIM, OWN), BF16),
            message,
            message,
            scratch=(*staged(OWN, message_rows, FACE), pltpu.SemaphoreType.DMA((2,))),
            raw=(0, 1),
        )(orbitals, cell_stiffness)
        far, near = swapped(far, near, gx, length_x)
        own_columns, partial, own_x, rim_x, face_x, own_y, side_y, face_y, edge_y = call(
            arrange,
            ((CELL, OWN), BF16),
            (by_orbital(CELL), F32),
            ((OWN, FACE), BF16),
            ((RIM, FACE), BF16),
            ((FACE, FACE), BF16),
            ((OWN, RIM), BF16),
            ((FACE, RIM), BF16),
            ((FACE, RIM), BF16),
            ((DEG, RIM), BF16),
            scratch=(pltpu.VMEM((CELL, CELL), F32),),
        )(stiffness, field)

        def row_part(partial, values, far, near):
            far, near, rim, above_x, raw = call(
                cross,
                message,
                message,
                (by_orbital(RIM), F32),
                (by_orbital(FACE), BF16),
                message,
                scratch=staged(message_rows, FACE, message_rows, message_rows),
            )(rim_x, face_x, partial, values, far, near)
            far, near = swapped(far, near, "gy", length_y)
            own = call(gather_row, (by_orbital(OWN), F32), scratch=staged(RIM, FACE))(
                own_x, face_y, edge_y, partial, values, above_x, rim, raw
            )[0]
            return own, far, near

        own, far, near = row_part(partial, field, far, near)
        lifted, far, near = call(
            lift,
            (by_orbital(OWN), BF16),
            message,
            message,
            scratch=staged(OWN, RIM, FACE, message_rows, message_rows),
        )(own_y, side_y, own, far, near, field, weight, rim_own)
        far, near = swapped(far, near, gx, length_x)

        def shuffle():
            place = lax.broadcasted_iota(jnp.int32, (orbital_count, 1), 0)
            low = lax.bitwise_and(place, quarter - 1)
            line = lax.shift_right_logical(low, block_rows.bit_length() - 1)
            side = lax.shift_right_logical(place, quarter.bit_length() - 1)
            order = (
                line * (4 * block_rows)
                + lax.bitwise_and(side, 1) * (2 * block_rows)
                + lax.shift_right_logical(side, 1) * block_rows
                + lax.bitwise_and(low, block_rows - 1)
            )
            return one_hot(order, orbital_count)

        def shuffled_product(own_columns, lifted, partial, order, shuffled):
            partial[...] = dot(own_columns[...], lifted[...])
            order[...] = shuffle()
            shuffled[...] = dot_columns(lifted[...], order[...]).astype(BF16)

        partial, order, shuffled = call(
            shuffled_product,
            (by_orbital(CELL), F32),
            ((orbital_count, orbital_count), BF16),
            (by_orbital(OWN), BF16),
        )(own_columns, lifted)
        own, far, near = row_part(partial, lifted, far, near)

        def filter_and_gram(
            own_y, side_y, own, far_in, near_in, field, lifted, potential, order, shuffled,
            filtered, keep, give, image, corner, face, wide, rows,
        ):
            core = lax.axis_index("core")

            def gram(which, left, right):
                product = (dot_rows(left, right) * norm_scale).astype(BF16)

                @pl.when(core == 0)
                def _():
                    keep[which] = product[:, :half]
                    give[which] = product[:, half:]

                @pl.when(core == 1)
                def _():
                    keep[which] = product[:, half:]
                    give[which] = product[:, :half]

            close(own_y, side_y, own, far_in, near_in, image, corner, face, wide)
            image[OWN:, :] = jnp.zeros((padded - OWN, orbital_count), F32)
            rows[OWN:, :] = jnp.zeros((padded - OWN, orbital_count), F32)
            rows[:OWN, :] = shuffled[...].astype(F32)
            lifted32 = lifted[...].astype(F32)
            image[:OWN, :] += potential[...] * lifted32
            gram(0, image[...].astype(BF16), rows[...].astype(BF16))
            image[:OWN, :] = (
                2.0 * (image[:OWN, :] - SPECTRUM_CENTER * lifted32) / SPECTRUM_HALF - field[...].astype(F32)
            )
            filtered[...] = image[:OWN, :].astype(BF16)
            values = image[...].astype(BF16)
            gram(1, values, dot_columns(values, order[...]).astype(BF16))

        half_grams = ((2, orbital_count, half), BF16)
        filtered, kept, given = call(
            filter_and_gram,
            (by_orbital(OWN), BF16),
            half_grams,
            half_grams,
            scratch=staged(padded, RIM, FACE, message_rows, padded),
            results=(0,),
        )(own_y, side_y, own, far, near, field, lifted, weight, order, shuffled)
        taken = lax.ppermute(given, "core", [(0, 1), (1, 0)])

        def pair_sum(kept, taken, out):
            for which in range(2):
                total = (kept[which].astype(F32) + taken[which].astype(F32)).astype(BF16)
                for side in range(2):
                    part = total[:, side * quarter : (side + 1) * quarter]
                    for j in range(length_y):
                        out[side, j, which * block_cols : (which + 1) * block_cols] = part[
                            j * block_cols : (j + 1) * block_cols
                        ]

        wide = 2 * block_cols
        fold = max(1, 128 // wide)
        short = block_rows // fold

        def plane_sum(terms, out):
            total = terms[0].astype(F32)
            for source in range(1, 2 * length_y):
                total += terms[source].astype(F32)
            total = total.T.reshape(length_z, block_rows, wide)
            for part in range(fold):
                out[:, :, part * wide : (part + 1) * wide] = total[:, part * short : (part + 1) * short, :].astype(BF16)

        def line_sum(terms, ham, correlation):
            total = terms[0].astype(F32)
            for source in range(1, length_z):
                total += terms[source].astype(F32)
            for part in range(fold):
                block = total[:, part * wide : (part + 1) * wide]
                ham[part * short : (part + 1) * short, :] = block[:, :block_cols]
                correlation[part * short : (part + 1) * short, :] = block[:, block_cols:]

        terms = call(pair_sum, ((2, length_y, wide, quarter), BF16))(kept, taken)[0]
        terms = terms.reshape(2 * length_y, wide, quarter)
        terms = lax.all_to_all(terms, ("half", "gy"), 0, 0, tiled=True)
        terms = call(plane_sum, ((length_z, short, fold * wide), BF16))(terms)[0]
        terms = lax.all_to_all(terms, "z", 0, 0, tiled=True)
        block = (block_rows, block_cols)
        projected_ham, correlation = call(line_sum, (block, F32), (block, F32), results=(0, 1))(terms)
        return filtered, projected_ham, correlation

    return jax.shard_map(
        per_device,
        mesh=split_mesh,
        in_specs=(P(every, None), P(every), P()),
        out_specs=(P(every, None), P(gx, "gy"), P(gx, "gy")),
        check_vma=False,
    )
```

```python
import math

import jax
import jax.numpy as jnp
from jax import lax
from jax.experimental import pallas as pl
from jax.experimental.pallas import tpu as pltpu
from jax.sharding import Mesh, PartitionSpec as P

DEG = 7
SIDE = DEG + 1
FACE = DEG * DEG
RIM = FACE + DEG
OWN = FACE * DEG
CELL = OWN + RIM + FACE
SPECTRUM_CENTER = 2.0
SPECTRUM_HALF = 2.0
VMEM_LIMIT = 24 * 2**20
F32 = jnp.float32
BF16 = jnp.bfloat16


def dot(left, right):
    return jnp.dot(left, right, preferred_element_type=F32)


def dot_rows(left, right):
    return lax.dot_general(left, right, (((0,), (0,)), ((), ())), preferred_element_type=F32)


def dot_columns(left, right):
    return lax.dot_general(left, right, (((1,), (1,)), ((), ())), preferred_element_type=F32)


def one_hot(column, width):
    return (column == lax.broadcasted_iota(jnp.int32, (column.shape[0], width), 1)).astype(F32).astype(BF16)


def node_order(first, count):
    place = first + lax.broadcasted_iota(jnp.int32, (count, 1), 0)

    def seventh(n):
        return lax.shift_right_logical(n * 9363, 16)

    column = seventh(place)
    plane = seventh(column)
    own = plane * SIDE * SIDE + (column - plane * DEG) * SIDE + (place - column * DEG)
    rim = place - OWN
    rim = DEG * SIDE * SIDE + seventh(rim) * SIDE + (rim - seventh(rim) * DEG)
    face = place - OWN - RIM
    face = seventh(face) * SIDE * SIDE + DEG * SIDE + (face - seventh(face) * DEG)
    return jnp.where(place < OWN, own, jnp.where(place < OWN + RIM, rim, face))


def call(kernel, *shapes, scratch=(), results=(), raw=()):
    def run(*args):
        vmem = pl.BlockSpec(memory_space=pltpu.VMEM)
        places = [
            pl.BlockSpec(memory_space=pl.ANY)
            if i in raw
            else vmem
            for i in range(len(args))
        ]
        return pl.pallas_call(
            kernel,
            out_shape=[
                jax.ShapeDtypeStruct(*shape) if i in results else pltpu.VMEM(*shape) for i, shape in enumerate(shapes)
            ],
            in_specs=places,
            out_specs=[vmem] * len(shapes),
            scratch_shapes=list(scratch),
            compiler_params=pltpu.CompilerParams(vmem_limit_bytes=VMEM_LIMIT),
            name=kernel.__name__,
        )(
            *[
                pltpu.with_memory_space_constraint(arg, pltpu.HBM if i in raw else pltpu.VMEM)
                for i, arg in enumerate(args)
            ]
        )

    return run


def chosen(upper, messages, arrived):
    far, near = messages

    @pl.when(upper)
    def _():
        arrived(near, far)

    @pl.when(jnp.logical_not(upper))
    def _():
        arrived(far, near)


def send(upper, far, near, upward, downward):
    @pl.when(upper)
    def _():
        far[...] = upward[...].astype(BF16)
        near[: downward.shape[0], :] = downward[...].astype(BF16)

    @pl.when(jnp.logical_not(upper))
    def _():
        near[...] = upward[...].astype(BF16)
        far[: downward.shape[0], :] = downward[...].astype(BF16)


def stage_parts(values, stage):
    count = values.shape[0]
    high = values.astype(BF16).astype(F32)
    stage[:count, :] = high
    stage[count : 2 * count, :] = values - high


def stage_plane(values, stage, start):
    for i in range(DEG):
        stage[start + i * DEG : start + (i + 1) * DEG, :] = values[i * FACE : i * FACE + DEG, :]


def pack_x(rim, wide, far, near, upward, downward):
    upward[:RIM, :] = rim
    stage_plane(wide, upward, RIM)
    downward[...] = wide[:FACE, :]
    send(lax.axis_index("core") == 1, far, near, upward, downward)


def inside_x():
    return (lax.axis_index("z") + lax.axis_index("half") + lax.axis_index("core") > 0).astype(F32)


def inside_y():
    return (lax.axis_index("gy") > 0).astype(F32)


def prepare(field_in, stiffness_in, field, stiffness, rim_own, far, near, wide, upward, downward, sems):
    copies = [
        pltpu.make_async_copy(stiffness_in, stiffness, sems.at[0]),
        pltpu.make_async_copy(field_in, field, sems.at[1]),
    ]
    for copy in copies:
        copy.start()
    nodes = one_hot(node_order(0, OWN), SIDE**3)
    rim = one_hot(node_order(OWN, RIM), SIDE**3)
    copies[0].wait()
    rim_own[...] = dot_columns(dot(rim, stiffness[...]).astype(BF16), nodes).astype(BF16)
    copies[1].wait()
    wide[...] = field[...].astype(F32)
    pack_x(dot(rim_own[...], field[...]), wide, far, near, upward, downward)


def arrange(stiffness, field, own_columns, partial, own_x, rim_x, face_x, own_y, side_y, face_y, edge_y, ordered):
    order = one_hot(node_order(0, CELL), SIDE**3)
    ordered[...] = dot_columns(dot(order, stiffness[...]).astype(BF16), order)
    own_columns[...] = ordered[:, :OWN].astype(BF16)
    partial[...] = dot(own_columns[...], field[...])
    to_x, to_y = OWN, OWN + FACE
    own_x[...] = ordered[:OWN, to_x:to_y].astype(BF16)
    rim_x[...] = ordered[OWN : OWN + RIM, to_x:to_y].astype(BF16)
    face_x[...] = ordered[OWN + RIM :, to_x:to_y].astype(BF16)
    own_y[...] = ordered[:OWN, to_y:].astype(BF16)
    side_y[...] = ordered[OWN : OWN + FACE, to_y:].astype(BF16)
    face_y[...] = ordered[OWN + RIM :, to_y:].astype(BF16)
    edge_y[...] = ordered[OWN + FACE : OWN + RIM, to_y:].astype(BF16)


def cross(rim_x, face_x, partial, field, far_in, near_in, far, near, rim, above_x, raw, wide, face, upward, downward):
    def arrived(below, above):
        wide[...] = below[...].astype(F32)
        face[...] = above[:FACE, :].astype(F32)

    chosen(lax.axis_index("core") == 1, (far_in, near_in), arrived)
    above_x[...] = face[...].astype(BF16)
    rim[...] = wide[:RIM, :] + inside_x() * dot(rim_x[...], field[:FACE, :])
    row = partial[OWN + RIM :, :] + dot(face_x[...], above_x[...])
    downward[:DEG, :] = face[:DEG, :]
    stage_plane(field[...].astype(F32), downward, DEG)
    downward[RIM:, :] = wide[RIM:, :]
    wide[:FACE, :] = row
    wide[:DEG, :] += rim[FACE:, :]
    upward[...] = jnp.zeros_like(upward)
    stage_parts(wide[:FACE, :], upward)
    raw[...] = downward[...].astype(BF16)
    send(lax.bitwise_and(lax.axis_index("gy"), 1) == 1, far, near, upward, downward)


def gather_row(own_x, face_y, edge_y, partial, field, above_x, rim, raw, own, corner, face):
    own[...] = partial[:OWN, :] + dot(own_x[...], above_x[...])
    own[:FACE, :] += rim[:FACE, :]
    face[...] = inside_y() * dot(face_y[...], raw[:RIM, :])
    for i in range(DEG):
        own[i * FACE : i * FACE + DEG, :] += face[i * DEG : (i + 1) * DEG, :]
    wide = raw[...].astype(F32)
    corner[:DEG, :] = field[...].astype(F32)[:DEG]
    corner[DEG:, :] = wide[RIM:]
    own[:DEG, :] += inside_x() * inside_y() * dot(edge_y[...], corner[...].astype(BF16))


def close(own_y, side_y, own, far_in, near_in, image, corner, face, wide):
    def arrived(below, above):
        parts = below[...].astype(F32)
        face[...] = parts[:FACE, :] + parts[FACE : 2 * FACE, :]
        wide[...] = above[...].astype(F32)

    chosen(lax.bitwise_and(lax.axis_index("gy"), 1) == 1, (far_in, near_in), arrived)
    corner[:DEG, :] = wide[DEG : 2 * DEG, :]
    corner[DEG:, :] = wide[RIM:, :]
    image[:OWN, :] = own[...] + dot(own_y[...], wide[:RIM, :].astype(BF16))
    image[:FACE, :] += inside_x() * dot(side_y[...], corner[...].astype(BF16))
    for i in range(DEG):
        image[i * FACE : i * FACE + DEG, :] += face[i * DEG : (i + 1) * DEG, :]


def lift(
    own_y, side_y, own, far_in, near_in, field, potential, rim_own,
    lifted, far, near, image, corner, face, wide, upward,
):
    close(own_y, side_y, own, far_in, near_in, image, corner, face, wide)
    field32 = field[...].astype(F32)
    first_image = image[...] + potential[...] * field32
    image[...] = (first_image - SPECTRUM_CENTER * field32) / SPECTRUM_HALF
    lifted[...] = image[...].astype(BF16)
    pack_x(dot(rim_own[...], lifted[...]), image, far, near, upward, face)


def solution(mesh):
    length_x, length_y = mesh.shape["gx"], mesh.shape["gy"]
    length_z = length_x // 4
    split_mesh = Mesh(mesh.devices.reshape(length_z, 2, 2, length_y), ("z", "half", "core", "gy"))
    gx = ("z", "half", "core")
    every = gx + ("gy",)

    def swapped(far, near, axis, length):
        def pairs(first):
            return [(i + j, i + 1 - j) for i in range(first, length - 1, 2) for j in range(2)]

        return lax.ppermute(far, axis, pairs(1)), lax.ppermute(near, axis, pairs(0))

    def per_device(orbitals, potential, cell_stiffness):
        node_count, orbital_count = orbitals.shape
        norm_scale = 1.0 / math.sqrt(node_count * length_x * length_y)
        block_rows = orbital_count // length_x
        block_cols = orbital_count // length_y
        half = orbital_count // 2
        padded = -(-OWN // 128) * 128

        def by_orbital(rows):
            return (rows, orbital_count)

        def staged(*rows):
            return tuple(pltpu.VMEM(by_orbital(n), F32) for n in rows)

        weight = potential[:, None]
        message_rows = RIM + FACE
        message = (by_orbital(message_rows), BF16)

        field, stiffness, rim_own, far, near = call(
            prepare,
            (by_orbital(OWN), BF16),
            ((SIDE**3, SIDE**3), BF16),
            ((RIM, OWN), BF16),
            message,
            message,
            scratch=(*staged(OWN, message_rows, FACE), pltpu.SemaphoreType.DMA((2,))),
            raw=(0, 1),
        )(orbitals, cell_stiffness)
        far, near = swapped(far, near, gx, length_x)
        own_columns, partial, own_x, rim_x, face_x, own_y, side_y, face_y, edge_y = call(
            arrange,
            ((CELL, OWN), BF16),
            (by_orbital(CELL), F32),
            ((OWN, FACE), BF16),
            ((RIM, FACE), BF16),
            ((FACE, FACE), BF16),
            ((OWN, RIM), BF16),
            ((FACE, RIM), BF16),
            ((FACE, RIM), BF16),
            ((DEG, RIM), BF16),
            scratch=(pltpu.VMEM((CELL, CELL), F32),),
        )(stiffness, field)

        def row_part(partial, values, far, near):
            far, near, rim, above_x, raw = call(
                cross,
                message,
                message,
                (by_orbital(RIM), F32),
                (by_orbital(FACE), BF16),
                message,
                scratch=staged(message_rows, FACE, message_rows, message_rows),
            )(rim_x, face_x, partial, values, far, near)
            far, near = swapped(far, near, "gy", length_y)
            own = call(gather_row, (by_orbital(OWN), F32), scratch=staged(RIM, FACE))(
                own_x, face_y, edge_y, partial, values, above_x, rim, raw
            )[0]
            return own, far, near

        own, far, near = row_part(partial, field, far, near)
        lifted, far, near = call(
            lift,
            (by_orbital(OWN), BF16),
            message,
            message,
            scratch=staged(OWN, RIM, FACE, message_rows, message_rows),
        )(own_y, side_y, own, far, near, field, weight, rim_own)
        far, near = swapped(far, near, gx, length_x)

        def shuffle():
            place = lax.broadcasted_iota(jnp.int32, (orbital_count, 1), 0)
            block = lax.shift_right_logical(lax.bitwise_and(place, half - 1), block_rows.bit_length() - 1)
            side = lax.bitwise_xor(lax.shift_right_logical(place, half.bit_length() - 1), lax.axis_index("core"))
            order = block * (2 * block_rows) + side * block_rows + lax.bitwise_and(place, block_rows - 1)
            return one_hot(order, orbital_count)

        def shuffled_product(own_columns, lifted, partial, order, shuffled):
            partial[...] = dot(own_columns[...], lifted[...])
            order[...] = shuffle()
            shuffled[...] = dot_columns(lifted[...], order[...]).astype(BF16)

        partial, order, shuffled = call(
            shuffled_product,
            (by_orbital(CELL), F32),
            ((orbital_count, orbital_count), BF16),
            (by_orbital(OWN), BF16),
        )(own_columns, lifted)
        own, far, near = row_part(partial, lifted, far, near)

        def filter_and_gram(
            own_y, side_y, own, far_in, near_in, field, lifted, potential, order, shuffled,
            filtered, keep, give, image, corner, face, wide, rows,
        ):
            def gram(which, left, right):
                product = (dot_rows(left, right) * norm_scale).astype(BF16)
                keep[which] = product[:, :half]
                give[which] = product[:, half:]

            close(own_y, side_y, own, far_in, near_in, image, corner, face, wide)
            image[OWN:, :] = jnp.zeros((padded - OWN, orbital_count), F32)
            rows[OWN:, :] = jnp.zeros((padded - OWN, orbital_count), F32)
            rows[:OWN, :] = shuffled[...].astype(F32)
            lifted32 = lifted[...].astype(F32)
            image[:OWN, :] += potential[...] * lifted32
            gram(0, image[...].astype(BF16), rows[...].astype(BF16))
            image[:OWN, :] = (
                2.0 * (image[:OWN, :] - SPECTRUM_CENTER * lifted32) / SPECTRUM_HALF - field[...].astype(F32)
            )
            filtered[...] = image[:OWN, :].astype(BF16)
            values = image[...].astype(BF16)
            gram(1, values, dot_columns(values, order[...]).astype(BF16))

        half_grams = ((2, orbital_count, half), BF16)
        filtered, kept, given = call(
            filter_and_gram,
            (by_orbital(OWN), BF16),
            half_grams,
            half_grams,
            scratch=staged(padded, RIM, FACE, message_rows, padded),
            results=(0,),
        )(own_y, side_y, own, far, near, field, lifted, weight, order, shuffled)
        taken = lax.ppermute(given, "core", [(0, 1), (1, 0)])

        def pair_sum(kept, taken, out):
            for which in range(2):
                total = (kept[which].astype(F32) + taken[which].astype(F32)).astype(BF16)
                for j in range(length_y):
                    out[j, which * block_cols : (which + 1) * block_cols] = total[j * block_cols : (j + 1) * block_cols]

        wide = 2 * block_cols
        fold = max(1, 128 // wide)
        short = block_rows // fold

        def plane_sum(terms, out):
            total = terms[0].astype(F32)
            for source in range(1, length_y):
                total += terms[source].astype(F32)
            total = total.T.reshape(length_x // 2, block_rows, wide)
            for part in range(fold):
                out[:, :, part * wide : (part + 1) * wide] = total[:, part * short : (part + 1) * short, :].astype(BF16)

        def line_sum(terms, ham, correlation):
            total = terms[0].astype(F32)
            for source in range(1, length_x // 2):
                total += terms[source].astype(F32)
            for part in range(fold):
                block = total[:, part * wide : (part + 1) * wide]
                ham[part * short : (part + 1) * short, :] = block[:, :block_cols]
                correlation[part * short : (part + 1) * short, :] = block[:, block_cols:]

        terms = call(pair_sum, ((length_y, wide, half), BF16))(kept, taken)[0]
        terms = lax.all_to_all(terms, "gy", 0, 0, tiled=True)
        terms = call(plane_sum, ((length_x // 2, short, fold * wide), BF16))(terms)[0]
        terms = lax.all_to_all(terms, ("z", "half"), 0, 0, tiled=True)
        block = (block_rows, block_cols)
        projected_ham, correlation = call(line_sum, (block, F32), (block, F32), results=(0, 1))(terms)
        return filtered, projected_ham, correlation

    return jax.shard_map(
        per_device,
        mesh=split_mesh,
        in_specs=(P(every, None), P(every), P()),
        out_specs=(P(every, None), P(gx, "gy"), P(gx, "gy")),
        check_vma=False,
    )
```

```python
import math

import jax
import jax.numpy as jnp
from jax import lax
from jax.experimental import pallas as pl
from jax.experimental.pallas import tpu as pltpu
from jax.sharding import Mesh, PartitionSpec as P

DEG = 7
SIDE = DEG + 1
FACE = DEG * DEG
RIM = FACE + DEG
OWN = FACE * DEG
CELL = OWN + RIM + FACE
SPECTRUM_CENTER = 2.0
SPECTRUM_HALF = 2.0
VMEM_LIMIT = 24 * 2**20
F32 = jnp.float32
BF16 = jnp.bfloat16


def dot(left, right):
    return jnp.dot(left, right, preferred_element_type=F32)


def dot_rows(left, right):
    return lax.dot_general(left, right, (((0,), (0,)), ((), ())), preferred_element_type=F32)


def dot_columns(left, right):
    return lax.dot_general(left, right, (((1,), (1,)), ((), ())), preferred_element_type=F32)


def one_hot(column, width):
    return (column == lax.broadcasted_iota(jnp.int32, (column.shape[0], width), 1)).astype(F32).astype(BF16)


def node_order(first, count):
    place = first + lax.broadcasted_iota(jnp.int32, (count, 1), 0)

    def seventh(n):
        return lax.shift_right_logical(n * 9363, 16)

    column = seventh(place)
    plane = seventh(column)
    own = plane * SIDE * SIDE + (column - plane * DEG) * SIDE + (place - column * DEG)
    rim = place - OWN
    rim = DEG * SIDE * SIDE + seventh(rim) * SIDE + (rim - seventh(rim) * DEG)
    face = place - OWN - RIM
    face = seventh(face) * SIDE * SIDE + DEG * SIDE + (face - seventh(face) * DEG)
    return jnp.where(place < OWN, own, jnp.where(place < OWN + RIM, rim, face))


def call(kernel, *shapes, scratch=(), results=(), raw=()):
    def run(*args):
        vmem = pl.BlockSpec(memory_space=pltpu.VMEM)
        places = [
            pl.BlockSpec(memory_space=pl.ANY)
            if i in raw
            else vmem
            for i in range(len(args))
        ]
        return pl.pallas_call(
            kernel,
            out_shape=[
                jax.ShapeDtypeStruct(*shape) if i in results else pltpu.VMEM(*shape) for i, shape in enumerate(shapes)
            ],
            in_specs=places,
            out_specs=[vmem] * len(shapes),
            scratch_shapes=list(scratch),
            compiler_params=pltpu.CompilerParams(vmem_limit_bytes=VMEM_LIMIT),
            name=kernel.__name__,
        )(
            *[
                pltpu.with_memory_space_constraint(arg, pltpu.HBM if i in raw else pltpu.VMEM)
                for i, arg in enumerate(args)
            ]
        )

    return run


def chosen(upper, messages, arrived):
    far, near = messages

    @pl.when(upper)
    def _():
        arrived(near, far)

    @pl.when(jnp.logical_not(upper))
    def _():
        arrived(far, near)


def send(upper, far, near, upward, downward):
    @pl.when(upper)
    def _():
        far[...] = upward[...].astype(BF16)
        near[: downward.shape[0], :] = downward[...].astype(BF16)

    @pl.when(jnp.logical_not(upper))
    def _():
        near[...] = upward[...].astype(BF16)
        far[: downward.shape[0], :] = downward[...].astype(BF16)


def stage_parts(values, stage):
    count = values.shape[0]
    high = values.astype(BF16).astype(F32)
    stage[:count, :] = high
    stage[count : 2 * count, :] = values - high


def stage_plane(values, stage, start):
    for i in range(DEG):
        stage[start + i * DEG : start + (i + 1) * DEG, :] = values[i * FACE : i * FACE + DEG, :]


def pack_x(rim, wide, far, near, upward, downward):
    upward[:RIM, :] = rim
    stage_plane(wide, upward, RIM)
    downward[...] = wide[:FACE, :]
    send(lax.axis_index("core") == 1, far, near, upward, downward)


def inside_x():
    return (lax.axis_index("z") + lax.axis_index("half") + lax.axis_index("core") > 0).astype(F32)


def inside_y():
    return (lax.axis_index("gy") > 0).astype(F32)


def prepare(field_in, stiffness_in, field, stiffness, rim_own, far, near, wide, upward, downward, sems):
    copies = [
        pltpu.make_async_copy(stiffness_in, stiffness, sems.at[0]),
        pltpu.make_async_copy(field_in, field, sems.at[1]),
    ]
    for copy in copies:
        copy.start()
    nodes = one_hot(node_order(0, OWN), SIDE**3)
    rim = one_hot(node_order(OWN, RIM), SIDE**3)
    copies[0].wait()
    rim_own[...] = dot_columns(dot(rim, stiffness[...]).astype(BF16), nodes).astype(BF16)
    copies[1].wait()
    wide[...] = field[...].astype(F32)
    pack_x(dot(rim_own[...], field[...]), wide, far, near, upward, downward)


def arrange(stiffness, field, own_columns, partial, own_x, rim_x, face_x, own_y, side_y, face_y, edge_y, ordered):
    order = one_hot(node_order(0, CELL), SIDE**3)
    ordered[...] = dot_columns(dot(order, stiffness[...]).astype(BF16), order)
    own_columns[...] = ordered[:, :OWN].astype(BF16)
    partial[...] = dot(own_columns[...], field[...])
    to_x, to_y = OWN, OWN + FACE
    own_x[...] = ordered[:OWN, to_x:to_y].astype(BF16)
    rim_x[...] = ordered[OWN : OWN + RIM, to_x:to_y].astype(BF16)
    face_x[...] = ordered[OWN + RIM :, to_x:to_y].astype(BF16)
    own_y[...] = ordered[:OWN, to_y:].astype(BF16)
    side_y[...] = ordered[OWN : OWN + FACE, to_y:].astype(BF16)
    face_y[...] = ordered[OWN + RIM :, to_y:].astype(BF16)
    edge_y[...] = ordered[OWN + FACE : OWN + RIM, to_y:].astype(BF16)


def cross(rim_x, face_x, partial, field, far_in, near_in, far, near, rim, above_x, raw, wide, face, upward, downward):
    def arrived(below, above):
        wide[...] = below[...].astype(F32)
        face[...] = above[:FACE, :].astype(F32)

    chosen(lax.axis_index("core") == 1, (far_in, near_in), arrived)
    above_x[...] = face[...].astype(BF16)
    rim[...] = wide[:RIM, :] + inside_x() * dot(rim_x[...], field[:FACE, :])
    row = partial[OWN + RIM :, :] + dot(face_x[...], above_x[...])
    downward[:DEG, :] = face[:DEG, :]
    stage_plane(field[...].astype(F32), downward, DEG)
    downward[RIM:, :] = wide[RIM:, :]
    wide[:FACE, :] = row
    wide[:DEG, :] += rim[FACE:, :]
    upward[...] = jnp.zeros_like(upward)
    stage_parts(wide[:FACE, :], upward)
    raw[...] = downward[...].astype(BF16)
    send(lax.bitwise_and(lax.axis_index("gy"), 1) == 1, far, near, upward, downward)


def gather_row(own_x, face_y, edge_y, partial, field, above_x, rim, raw, own, corner, face):
    own[...] = partial[:OWN, :] + dot(own_x[...], above_x[...])
    own[:FACE, :] += rim[:FACE, :]
    face[...] = inside_y() * dot(face_y[...], raw[:RIM, :])
    for i in range(DEG):
        own[i * FACE : i * FACE + DEG, :] += face[i * DEG : (i + 1) * DEG, :]
    wide = raw[...].astype(F32)
    corner[:DEG, :] = field[...].astype(F32)[:DEG]
    corner[DEG:, :] = wide[RIM:]
    own[:DEG, :] += inside_x() * inside_y() * dot(edge_y[...], corner[...].astype(BF16))


def close(own_y, side_y, own, far_in, near_in, image, corner, face, wide):
    def arrived(below, above):
        parts = below[...].astype(F32)
        face[...] = parts[:FACE, :] + parts[FACE : 2 * FACE, :]
        wide[...] = above[...].astype(F32)

    chosen(lax.bitwise_and(lax.axis_index("gy"), 1) == 1, (far_in, near_in), arrived)
    corner[:DEG, :] = wide[DEG : 2 * DEG, :]
    corner[DEG:, :] = wide[RIM:, :]
    image[:OWN, :] = own[...] + dot(own_y[...], wide[:RIM, :].astype(BF16))
    image[:FACE, :] += inside_x() * dot(side_y[...], corner[...].astype(BF16))
    for i in range(DEG):
        image[i * FACE : i * FACE + DEG, :] += face[i * DEG : (i + 1) * DEG, :]


def lift(
    own_y, side_y, own, far_in, near_in, field, potential, rim_own,
    lifted, far, near, image, corner, face, wide, upward,
):
    close(own_y, side_y, own, far_in, near_in, image, corner, face, wide)
    field32 = field[...].astype(F32)
    first_image = image[...] + potential[...] * field32
    image[...] = (first_image - SPECTRUM_CENTER * field32) / SPECTRUM_HALF
    lifted[...] = image[...].astype(BF16)
    pack_x(dot(rim_own[...], lifted[...]), image, far, near, upward, face)


def solution(mesh):
    length_x, length_y = mesh.shape["gx"], mesh.shape["gy"]
    length_z = length_x // 4
    split_mesh = Mesh(mesh.devices.reshape(length_z, 2, 2, length_y), ("z", "half", "core", "gy"))
    gx = ("z", "half", "core")
    every = gx + ("gy",)

    def swapped(far, near, axis, length):
        def pairs(first):
            return [(i + j, i + 1 - j) for i in range(first, length - 1, 2) for j in range(2)]

        return lax.ppermute(far, axis, pairs(1)), lax.ppermute(near, axis, pairs(0))

    def per_device(orbitals, potential, cell_stiffness):
        node_count, orbital_count = orbitals.shape
        norm_scale = 1.0 / math.sqrt(node_count * length_x * length_y)
        block_rows = orbital_count // length_x
        block_cols = orbital_count // length_y
        half = orbital_count // 2
        quarter = orbital_count // 4
        padded = -(-OWN // 128) * 128

        def by_orbital(rows):
            return (rows, orbital_count)

        def staged(*rows):
            return tuple(pltpu.VMEM(by_orbital(n), F32) for n in rows)

        weight = potential[:, None]
        message_rows = RIM + FACE
        message = (by_orbital(message_rows), BF16)

        field, stiffness, rim_own, far, near = call(
            prepare,
            (by_orbital(OWN), BF16),
            ((SIDE**3, SIDE**3), BF16),
            ((RIM, OWN), BF16),
            message,
            message,
            scratch=(*staged(OWN, message_rows, FACE), pltpu.SemaphoreType.DMA((2,))),
            raw=(0, 1),
        )(orbitals, cell_stiffness)
        far, near = swapped(far, near, gx, length_x)
        own_columns, partial, own_x, rim_x, face_x, own_y, side_y, face_y, edge_y = call(
            arrange,
            ((CELL, OWN), BF16),
            (by_orbital(CELL), F32),
            ((OWN, FACE), BF16),
            ((RIM, FACE), BF16),
            ((FACE, FACE), BF16),
            ((OWN, RIM), BF16),
            ((FACE, RIM), BF16),
            ((FACE, RIM), BF16),
            ((DEG, RIM), BF16),
            scratch=(pltpu.VMEM((CELL, CELL), F32),),
        )(stiffness, field)

        def row_part(partial, values, far, near):
            far, near, rim, above_x, raw = call(
                cross,
                message,
                message,
                (by_orbital(RIM), F32),
                (by_orbital(FACE), BF16),
                message,
                scratch=staged(message_rows, FACE, message_rows, message_rows),
            )(rim_x, face_x, partial, values, far, near)
            far, near = swapped(far, near, "gy", length_y)
            own = call(gather_row, (by_orbital(OWN), F32), scratch=staged(RIM, FACE))(
                own_x, face_y, edge_y, partial, values, above_x, rim, raw
            )[0]
            return own, far, near

        own, far, near = row_part(partial, field, far, near)
        lifted, far, near = call(
            lift,
            (by_orbital(OWN), BF16),
            message,
            message,
            scratch=staged(OWN, RIM, FACE, message_rows, message_rows),
        )(own_y, side_y, own, far, near, field, weight, rim_own)
        far, near = swapped(far, near, gx, length_x)

        def shuffle():
            place = lax.broadcasted_iota(jnp.int32, (orbital_count, 1), 0)
            line = lax.shift_right_logical(lax.bitwise_and(place, quarter - 1), block_rows.bit_length() - 1)
            side = lax.shift_right_logical(place, quarter.bit_length() - 1)
            core = lax.bitwise_xor(lax.shift_right_logical(side, 1), lax.axis_index("core"))
            block = line * 4 + lax.bitwise_and(side, 1) * 2 + core
            order = block * block_rows + lax.bitwise_and(place, block_rows - 1)
            return one_hot(order, orbital_count)

        def shuffled_product(own_columns, lifted, partial, order, shuffled):
            partial[...] = dot(own_columns[...], lifted[...])
            order[...] = shuffle()
            shuffled[...] = dot_columns(lifted[...], order[...]).astype(BF16)

        partial, order, shuffled = call(
            shuffled_product,
            (by_orbital(CELL), F32),
            ((orbital_count, orbital_count), BF16),
            (by_orbital(OWN), BF16),
        )(own_columns, lifted)
        own, far, near = row_part(partial, lifted, far, near)

        def filter_and_gram(
            own_y, side_y, own, far_in, near_in, field, lifted, potential, order, shuffled,
            filtered, keep, give, image, corner, face, wide, rows,
        ):
            def gram(which, left, right):
                product = (dot_rows(left, right) * norm_scale).astype(BF16)
                keep[which] = product[:, :half]
                give[which] = product[:, half:]

            close(own_y, side_y, own, far_in, near_in, image, corner, face, wide)
            image[OWN:, :] = jnp.zeros((padded - OWN, orbital_count), F32)
            rows[OWN:, :] = jnp.zeros((padded - OWN, orbital_count), F32)
            rows[:OWN, :] = shuffled[...].astype(F32)
            lifted32 = lifted[...].astype(F32)
            image[:OWN, :] += potential[...] * lifted32
            gram(0, image[...].astype(BF16), rows[...].astype(BF16))
            image[:OWN, :] = (
                2.0 * (image[:OWN, :] - SPECTRUM_CENTER * lifted32) / SPECTRUM_HALF - field[...].astype(F32)
            )
            filtered[...] = image[:OWN, :].astype(BF16)
            values = image[...].astype(BF16)
            gram(1, values, dot_columns(values, order[...]).astype(BF16))

        half_grams = ((2, orbital_count, half), BF16)
        filtered, kept, given = call(
            filter_and_gram,
            (by_orbital(OWN), BF16),
            half_grams,
            half_grams,
            scratch=staged(padded, RIM, FACE, message_rows, padded),
        )(own_y, side_y, own, far, near, field, lifted, weight, order, shuffled)
        taken = lax.ppermute(given, "core", [(0, 1), (1, 0)])

        def pair_sum(kept, taken, out):
            for which in range(2):
                total = (kept[which].astype(F32) + taken[which].astype(F32)).astype(BF16)
                for side in range(2):
                    part = total[:, side * quarter : (side + 1) * quarter]
                    for j in range(length_y):
                        out[side, j, which * block_cols : (which + 1) * block_cols] = part[
                            j * block_cols : (j + 1) * block_cols
                        ]

        wide = 2 * block_cols
        fold = max(1, 128 // wide)
        short = block_rows // fold

        def plane_sum(terms, out):
            total = terms[0].astype(F32)
            for source in range(1, 2 * length_y):
                total += terms[source].astype(F32)
            total = total.T.reshape(length_z, block_rows, wide)
            for part in range(fold):
                out[:, :, part * wide : (part + 1) * wide] = total[:, part * short : (part + 1) * short, :].astype(BF16)

        def line_sum(terms, ham, correlation):
            total = terms[0].astype(F32)
            for source in range(1, length_z):
                total += terms[source].astype(F32)
            for part in range(fold):
                block = total[:, part * wide : (part + 1) * wide]
                ham[part * short : (part + 1) * short, :] = block[:, :block_cols]
                correlation[part * short : (part + 1) * short, :] = block[:, block_cols:]

        terms = call(pair_sum, ((2, length_y, wide, quarter), BF16))(kept, taken)[0]
        terms = terms.reshape(2 * length_y, wide, quarter)
        terms = lax.all_to_all(terms, ("half", "gy"), 0, 0, tiled=True)
        terms = call(plane_sum, ((length_z, short, fold * wide), BF16))(terms)[0]
        terms = lax.all_to_all(terms, "z", 0, 0, tiled=True)
        block = (block_rows, block_cols)
        projected_ham, correlation = call(line_sum, (block, F32), (block, F32), results=(0, 1))(terms)
        return filtered, projected_ham, correlation

    return jax.shard_map(
        per_device,
        mesh=split_mesh,
        in_specs=(P(every, None), P(every), P()),
        out_specs=(P(every, None), P(gx, "gy"), P(gx, "gy")),
        check_vma=False,
    )
```

```python
import math

import jax
import jax.numpy as jnp
from jax import lax
from jax.experimental import pallas as pl
from jax.experimental.pallas import tpu as pltpu
from jax.sharding import Mesh, PartitionSpec as P

DEG = 7
SIDE = DEG + 1
FACE = DEG * DEG
RIM = FACE + DEG
OWN = FACE * DEG
CELL = OWN + RIM + FACE
SPECTRUM_CENTER = 2.0
SPECTRUM_HALF = 2.0
VMEM_LIMIT = 24 * 2**20
F32 = jnp.float32
BF16 = jnp.bfloat16


def dot(left, right):
    return jnp.dot(left, right, preferred_element_type=F32)


def dot_rows(left, right):
    return lax.dot_general(left, right, (((0,), (0,)), ((), ())), preferred_element_type=F32)


def dot_columns(left, right):
    return lax.dot_general(left, right, (((1,), (1,)), ((), ())), preferred_element_type=F32)


def one_hot(column, width):
    return (column == lax.broadcasted_iota(jnp.int32, (column.shape[0], width), 1)).astype(F32).astype(BF16)


def node_order(first, count):
    place = first + lax.broadcasted_iota(jnp.int32, (count, 1), 0)

    def seventh(n):
        return lax.shift_right_logical(n * 9363, 16)

    column = seventh(place)
    plane = seventh(column)
    own = plane * SIDE * SIDE + (column - plane * DEG) * SIDE + (place - column * DEG)
    rim = place - OWN
    rim = DEG * SIDE * SIDE + seventh(rim) * SIDE + (rim - seventh(rim) * DEG)
    face = place - OWN - RIM
    face = seventh(face) * SIDE * SIDE + DEG * SIDE + (face - seventh(face) * DEG)
    return jnp.where(place < OWN, own, jnp.where(place < OWN + RIM, rim, face))


def call(kernel, *shapes, scratch=(), results=(), raw=()):
    def run(*args):
        vmem = pl.BlockSpec(memory_space=pltpu.VMEM)
        places = [
            pl.BlockSpec(memory_space=pl.ANY)
            if i in raw
            else vmem
            for i in range(len(args))
        ]
        return pl.pallas_call(
            kernel,
            out_shape=[
                jax.ShapeDtypeStruct(*shape) if i in results else pltpu.VMEM(*shape) for i, shape in enumerate(shapes)
            ],
            in_specs=places,
            out_specs=[vmem] * len(shapes),
            scratch_shapes=list(scratch),
            compiler_params=pltpu.CompilerParams(vmem_limit_bytes=VMEM_LIMIT),
            name=kernel.__name__,
        )(
            *[
                pltpu.with_memory_space_constraint(arg, pltpu.HBM if i in raw else pltpu.VMEM)
                for i, arg in enumerate(args)
            ]
        )

    return run


def chosen(upper, messages, arrived):
    far, near = messages

    @pl.when(upper)
    def _():
        arrived(near, far)

    @pl.when(jnp.logical_not(upper))
    def _():
        arrived(far, near)


def send(upper, far, near, upward, downward):
    @pl.when(upper)
    def _():
        far[...] = upward[...].astype(BF16)
        near[: downward.shape[0], :] = downward[...].astype(BF16)

    @pl.when(jnp.logical_not(upper))
    def _():
        near[...] = upward[...].astype(BF16)
        far[: downward.shape[0], :] = downward[...].astype(BF16)


def stage_parts(values, stage):
    count = values.shape[0]
    high = values.astype(BF16).astype(F32)
    stage[:count, :] = high
    stage[count : 2 * count, :] = values - high


def stage_plane(values, stage, start):
    for i in range(DEG):
        stage[start + i * DEG : start + (i + 1) * DEG, :] = values[i * FACE : i * FACE + DEG, :]


def pack_x(rim, wide, far, near, upward, downward):
    upward[:RIM, :] = rim
    stage_plane(wide, upward, RIM)
    downward[...] = wide[:FACE, :]
    send(lax.axis_index("core") == 1, far, near, upward, downward)


def inside_x():
    return (lax.axis_index("z") + lax.axis_index("half") + lax.axis_index("core") > 0).astype(F32)


def inside_y():
    return (lax.axis_index("gy") > 0).astype(F32)


def prepare(field_in, stiffness_in, field, stiffness, rim_own, far, near, wide, upward, downward, sems):
    copies = [
        pltpu.make_async_copy(stiffness_in, stiffness, sems.at[0]),
        pltpu.make_async_copy(field_in, field, sems.at[1]),
    ]
    for copy in copies:
        copy.start()
    nodes = one_hot(node_order(0, OWN), SIDE**3)
    rim = one_hot(node_order(OWN, RIM), SIDE**3)
    copies[0].wait()
    rim_own[...] = dot_columns(dot(rim, stiffness[...]).astype(BF16), nodes).astype(BF16)
    copies[1].wait()
    wide[...] = field[...].astype(F32)
    pack_x(dot(rim_own[...], field[...]), wide, far, near, upward, downward)


def arrange(stiffness, field, own_columns, partial, own_x, rim_x, face_x, own_y, side_y, face_y, edge_y, ordered):
    order = one_hot(node_order(0, CELL), SIDE**3)
    ordered[...] = dot_columns(dot(order, stiffness[...]).astype(BF16), order)
    own_columns[...] = ordered[:, :OWN].astype(BF16)
    partial[...] = dot(own_columns[...], field[...])
    to_x, to_y = OWN, OWN + FACE
    own_x[...] = ordered[:OWN, to_x:to_y].astype(BF16)
    rim_x[...] = ordered[OWN : OWN + RIM, to_x:to_y].astype(BF16)
    face_x[...] = ordered[OWN + RIM :, to_x:to_y].astype(BF16)
    own_y[...] = ordered[:OWN, to_y:].astype(BF16)
    side_y[...] = ordered[OWN : OWN + FACE, to_y:].astype(BF16)
    face_y[...] = ordered[OWN + RIM :, to_y:].astype(BF16)
    edge_y[...] = ordered[OWN + FACE : OWN + RIM, to_y:].astype(BF16)


def cross(rim_x, face_x, partial, field, far_in, near_in, far, near, rim, above_x, raw, wide, face, upward, downward):
    def arrived(below, above):
        wide[...] = below[...].astype(F32)
        face[...] = above[:FACE, :].astype(F32)

    chosen(lax.axis_index("core") == 1, (far_in, near_in), arrived)
    above_x[...] = face[...].astype(BF16)
    rim[...] = wide[:RIM, :] + inside_x() * dot(rim_x[...], field[:FACE, :])
    row = partial[OWN + RIM :, :] + dot(face_x[...], above_x[...])
    downward[:DEG, :] = face[:DEG, :]
    stage_plane(field[...].astype(F32), downward, DEG)
    downward[RIM:, :] = wide[RIM:, :]
    wide[:FACE, :] = row
    wide[:DEG, :] += rim[FACE:, :]
    upward[...] = jnp.zeros_like(upward)
    stage_parts(wide[:FACE, :], upward)
    raw[...] = downward[...].astype(BF16)
    send(lax.bitwise_and(lax.axis_index("gy"), 1) == 1, far, near, upward, downward)


def gather_row(own_x, face_y, edge_y, partial, field, above_x, rim, raw, own, corner, face):
    own[...] = partial[:OWN, :] + dot(own_x[...], above_x[...])
    own[:FACE, :] += rim[:FACE, :]
    face[...] = inside_y() * dot(face_y[...], raw[:RIM, :])
    for i in range(DEG):
        own[i * FACE : i * FACE + DEG, :] += face[i * DEG : (i + 1) * DEG, :]
    wide = raw[...].astype(F32)
    corner[:DEG, :] = field[...].astype(F32)[:DEG]
    corner[DEG:, :] = wide[RIM:]
    own[:DEG, :] += inside_x() * inside_y() * dot(edge_y[...], corner[...].astype(BF16))


def close(own_y, side_y, own, far_in, near_in, image, corner, face, wide):
    def arrived(below, above):
        parts = below[...].astype(F32)
        face[...] = parts[:FACE, :] + parts[FACE : 2 * FACE, :]
        wide[...] = above[...].astype(F32)

    chosen(lax.bitwise_and(lax.axis_index("gy"), 1) == 1, (far_in, near_in), arrived)
    corner[:DEG, :] = wide[DEG : 2 * DEG, :]
    corner[DEG:, :] = wide[RIM:, :]
    image[:OWN, :] = own[...] + dot(own_y[...], wide[:RIM, :].astype(BF16))
    image[:FACE, :] += inside_x() * dot(side_y[...], corner[...].astype(BF16))
    for i in range(DEG):
        image[i * FACE : i * FACE + DEG, :] += face[i * DEG : (i + 1) * DEG, :]


def lift(
    own_y, side_y, own, far_in, near_in, field, potential, rim_own,
    lifted, far, near, image, corner, face, wide, upward,
):
    close(own_y, side_y, own, far_in, near_in, image, corner, face, wide)
    field32 = field[...].astype(F32)
    first_image = image[...] + potential[...] * field32
    image[...] = (first_image - SPECTRUM_CENTER * field32) / SPECTRUM_HALF
    lifted[...] = image[...].astype(BF16)
    pack_x(dot(rim_own[...], lifted[...]), image, far, near, upward, face)


def solution(mesh):
    length_x, length_y = mesh.shape["gx"], mesh.shape["gy"]
    length_z = length_x // 4
    split_mesh = Mesh(mesh.devices.reshape(length_z, 2, 2, length_y), ("z", "half", "core", "gy"))
    gx = ("z", "half", "core")
    every = gx + ("gy",)

    def swapped(far, near, axis, length):
        def pairs(first):
            return [(i + j, i + 1 - j) for i in range(first, length - 1, 2) for j in range(2)]

        return lax.ppermute(far, axis, pairs(1)), lax.ppermute(near, axis, pairs(0))

    def per_device(orbitals, potential, cell_stiffness):
        node_count, orbital_count = orbitals.shape
        norm_scale = 1.0 / math.sqrt(node_count * length_x * length_y)
        block_rows = orbital_count // length_x
        block_cols = orbital_count // length_y
        half = orbital_count // 2
        quarter = orbital_count // 4
        padded = -(-OWN // 128) * 128

        def by_orbital(rows):
            return (rows, orbital_count)

        def staged(*rows):
            return tuple(pltpu.VMEM(by_orbital(n), F32) for n in rows)

        weight = potential[:, None]
        message_rows = RIM + FACE
        message = (by_orbital(message_rows), BF16)

        field, stiffness, rim_own, far, near = call(
            prepare,
            (by_orbital(OWN), BF16),
            ((SIDE**3, SIDE**3), BF16),
            ((RIM, OWN), BF16),
            message,
            message,
            scratch=(*staged(OWN, message_rows, FACE), pltpu.SemaphoreType.DMA((2,))),
            raw=(0, 1),
        )(orbitals, cell_stiffness)
        far, near = swapped(far, near, gx, length_x)
        own_columns, partial, own_x, rim_x, face_x, own_y, side_y, face_y, edge_y = call(
            arrange,
            ((CELL, OWN), BF16),
            (by_orbital(CELL), F32),
            ((OWN, FACE), BF16),
            ((RIM, FACE), BF16),
            ((FACE, FACE), BF16),
            ((OWN, RIM), BF16),
            ((FACE, RIM), BF16),
            ((FACE, RIM), BF16),
            ((DEG, RIM), BF16),
            scratch=(pltpu.VMEM((CELL, CELL), F32),),
        )(stiffness, field)

        def row_part(partial, values, far, near):
            far, near, rim, above_x, raw = call(
                cross,
                message,
                message,
                (by_orbital(RIM), F32),
                (by_orbital(FACE), BF16),
                message,
                scratch=staged(message_rows, FACE, message_rows, message_rows),
            )(rim_x, face_x, partial, values, far, near)
            far, near = swapped(far, near, "gy", length_y)
            own = call(gather_row, (by_orbital(OWN), F32), scratch=staged(RIM, FACE))(
                own_x, face_y, edge_y, partial, values, above_x, rim, raw
            )[0]
            return own, far, near

        own, far, near = row_part(partial, field, far, near)
        lifted, far, near = call(
            lift,
            (by_orbital(OWN), BF16),
            message,
            message,
            scratch=staged(OWN, RIM, FACE, message_rows, message_rows),
        )(own_y, side_y, own, far, near, field, weight, rim_own)
        far, near = swapped(far, near, gx, length_x)

        def shuffle():
            place = lax.broadcasted_iota(jnp.int32, (orbital_count, 1), 0)
            line = lax.shift_right_logical(lax.bitwise_and(place, quarter - 1), block_rows.bit_length() - 1)
            side = lax.shift_right_logical(place, quarter.bit_length() - 1)
            core = lax.bitwise_xor(lax.shift_right_logical(side, 1), lax.axis_index("core"))
            block = line * 4 + lax.bitwise_and(side, 1) * 2 + core
            order = block * block_rows + lax.bitwise_and(place, block_rows - 1)
            return one_hot(order, orbital_count)

        def shuffled_product(own_columns, lifted, partial, order, shuffled):
            partial[...] = dot(own_columns[...], lifted[...])
            order[...] = shuffle()
            shuffled[...] = dot_columns(lifted[...], order[...]).astype(BF16)

        partial, order, shuffled = call(
            shuffled_product,
            (by_orbital(CELL), F32),
            ((orbital_count, orbital_count), BF16),
            (by_orbital(OWN), BF16),
        )(own_columns, lifted)
        own, far, near = row_part(partial, lifted, far, near)

        def filter_and_gram(
            own_y, side_y, own, far_in, near_in, field, lifted, potential, order, shuffled,
            filtered, keep, give, image, corner, face, wide, rows,
        ):
            def gram(which, left, right):
                product = (dot_rows(left, right) * norm_scale).astype(BF16)
                keep[which] = product[:, :half]
                give[which] = product[:, half:]

            close(own_y, side_y, own, far_in, near_in, image, corner, face, wide)
            image[OWN:, :] = jnp.zeros((padded - OWN, orbital_count), F32)
            rows[OWN:, :] = jnp.zeros((padded - OWN, orbital_count), F32)
            rows[:OWN, :] = shuffled[...].astype(F32)
            lifted32 = lifted[...].astype(F32)
            image[:OWN, :] += potential[...] * lifted32
            gram(0, image[...].astype(BF16), rows[...].astype(BF16))
            image[:OWN, :] = (
                2.0 * (image[:OWN, :] - SPECTRUM_CENTER * lifted32) / SPECTRUM_HALF - field[...].astype(F32)
            )
            filtered[...] = image[:OWN, :].astype(BF16)
            values = image[...].astype(BF16)
            gram(1, values, dot_columns(values, order[...]).astype(BF16))

        half_grams = ((2, orbital_count, half), BF16)
        filtered, kept, given = call(
            filter_and_gram,
            (by_orbital(OWN), BF16),
            half_grams,
            half_grams,
            scratch=staged(padded, RIM, FACE, message_rows, padded),
            results=(0,),
        )(own_y, side_y, own, far, near, field, lifted, weight, order, shuffled)
        taken = lax.ppermute(given, "core", [(0, 1), (1, 0)])

        def pair_sum(kept, taken, out):
            for which in range(2):
                total = (kept[which].astype(F32) + taken[which].astype(F32)).astype(BF16)
                for side in range(2):
                    part = total[:, side * quarter : (side + 1) * quarter]
                    for j in range(length_y):
                        out[side, j, which * block_cols : (which + 1) * block_cols] = part[
                            j * block_cols : (j + 1) * block_cols
                        ]

        wide = 2 * block_cols
        fold = max(1, 128 // wide)
        short = block_rows // fold

        def plane_sum(terms, out):
            total = terms[0].astype(F32)
            for source in range(1, 2 * length_y):
                total += terms[source].astype(F32)
            total = total.T.reshape(length_z, block_rows, wide)
            for part in range(fold):
                out[:, :, part * wide : (part + 1) * wide] = total[:, part * short : (part + 1) * short, :].astype(BF16)

        def line_sum(terms, ham, correlation):
            total = terms[0].astype(F32)
            for source in range(1, length_z):
                total += terms[source].astype(F32)
            for part in range(fold):
                block = total[:, part * wide : (part + 1) * wide]
                ham[part * short : (part + 1) * short, :] = block[:, :block_cols]
                correlation[part * short : (part + 1) * short, :] = block[:, block_cols:]

        terms = call(pair_sum, ((2, length_y, wide, quarter), BF16))(kept, taken)[0]
        terms = terms.reshape(2 * length_y, wide, quarter)
        terms = lax.all_to_all(terms, ("half", "gy"), 0, 0, tiled=True)
        terms = call(plane_sum, ((length_z, short, fold * wide), BF16))(terms)[0]
        terms = lax.all_to_all(terms, "z", 0, 0, tiled=True)
        block = (block_rows, block_cols)
        projected_ham, correlation = call(line_sum, (block, F32), (block, F32), results=(0, 1))(terms)
        return filtered, projected_ham, correlation

    return jax.shard_map(
        per_device,
        mesh=split_mesh,
        in_specs=(P(every, None), P(every), P()),
        out_specs=(P(every, None), P(gx, "gy"), P(gx, "gy")),
        check_vma=False,
    )
```

```python
import math

import jax
import jax.numpy as jnp
from jax import lax
from jax.experimental import pallas as pl
from jax.experimental.pallas import tpu as pltpu
from jax.sharding import Mesh, PartitionSpec as P

DEG = 7
SIDE = DEG + 1
FACE = DEG * DEG
RIM = FACE + DEG
OWN = FACE * DEG
CELL = OWN + RIM + FACE
SPECTRUM_CENTER = 2.0
SPECTRUM_HALF = 2.0
VMEM_LIMIT = 24 * 2**20
F32 = jnp.float32
BF16 = jnp.bfloat16


def dot(left, right):
    return jnp.dot(left, right, preferred_element_type=F32)


def dot_rows(left, right):
    return lax.dot_general(left, right, (((0,), (0,)), ((), ())), preferred_element_type=F32)


def dot_columns(left, right):
    return lax.dot_general(left, right, (((1,), (1,)), ((), ())), preferred_element_type=F32)


def one_hot(column, width):
    return (column == lax.broadcasted_iota(jnp.int32, (column.shape[0], width), 1)).astype(F32).astype(BF16)


def node_order(first, count):
    place = first + lax.broadcasted_iota(jnp.int32, (count, 1), 0)

    def seventh(n):
        return lax.shift_right_logical(n * 9363, 16)

    column = seventh(place)
    plane = seventh(column)
    own = plane * SIDE * SIDE + (column - plane * DEG) * SIDE + (place - column * DEG)
    rim = place - OWN
    rim = DEG * SIDE * SIDE + seventh(rim) * SIDE + (rim - seventh(rim) * DEG)
    face = place - OWN - RIM
    face = seventh(face) * SIDE * SIDE + DEG * SIDE + (face - seventh(face) * DEG)
    return jnp.where(place < OWN, own, jnp.where(place < OWN + RIM, rim, face))


def call(kernel, *shapes, scratch=(), results=(), raw=()):
    def run(*args):
        vmem = pl.BlockSpec(memory_space=pltpu.VMEM)
        places = [
            pl.BlockSpec(memory_space=pl.ANY)
            if i in raw
            else vmem
            for i in range(len(args))
        ]
        return pl.pallas_call(
            kernel,
            out_shape=[
                jax.ShapeDtypeStruct(*shape) if i in results else pltpu.VMEM(*shape) for i, shape in enumerate(shapes)
            ],
            in_specs=places,
            out_specs=[vmem] * len(shapes),
            scratch_shapes=list(scratch),
            compiler_params=pltpu.CompilerParams(vmem_limit_bytes=VMEM_LIMIT),
            name=kernel.__name__,
        )(
            *[
                pltpu.with_memory_space_constraint(arg, pltpu.HBM if i in raw else pltpu.VMEM)
                for i, arg in enumerate(args)
            ]
        )

    return run


def chosen(upper, messages, arrived):
    far, near = messages

    @pl.when(upper)
    def _():
        arrived(near, far)

    @pl.when(jnp.logical_not(upper))
    def _():
        arrived(far, near)


def send(upper, far, near, upward, downward):
    @pl.when(upper)
    def _():
        far[...] = upward[...].astype(BF16)
        near[: downward.shape[0], :] = downward[...].astype(BF16)

    @pl.when(jnp.logical_not(upper))
    def _():
        near[...] = upward[...].astype(BF16)
        far[: downward.shape[0], :] = downward[...].astype(BF16)


def stage_parts(values, stage):
    count = values.shape[0]
    high = values.astype(BF16).astype(F32)
    stage[:count, :] = high
    stage[count : 2 * count, :] = values - high


def stage_plane(values, stage, start):
    for i in range(DEG):
        stage[start + i * DEG : start + (i + 1) * DEG, :] = values[i * FACE : i * FACE + DEG, :]


def pack_x(rim, wide, far, near, upward, downward):
    upward[:RIM, :] = rim
    stage_plane(wide, upward, RIM)
    downward[...] = wide[:FACE, :]
    send(lax.axis_index("core") == 1, far, near, upward, downward)


def inside_x():
    return (lax.axis_index("z") + lax.axis_index("half") + lax.axis_index("core") > 0).astype(F32)


def inside_y():
    return (lax.axis_index("row") + lax.axis_index("line") > 0).astype(F32)


def prepare(field_in, stiffness_in, field, stiffness, rim_own, far, near, wide, upward, downward, sems):
    copies = [
        pltpu.make_async_copy(stiffness_in, stiffness, sems.at[0]),
        pltpu.make_async_copy(field_in, field, sems.at[1]),
    ]
    for copy in copies:
        copy.start()
    nodes = one_hot(node_order(0, OWN), SIDE**3)
    rim = one_hot(node_order(OWN, RIM), SIDE**3)
    copies[0].wait()
    rim_own[...] = dot_columns(dot(rim, stiffness[...]).astype(BF16), nodes).astype(BF16)
    copies[1].wait()
    wide[...] = field[...].astype(F32)
    pack_x(dot(rim_own[...], field[...]), wide, far, near, upward, downward)


def arrange(stiffness, field, own_columns, partial, own_x, rim_x, face_x, own_y, side_y, face_y, edge_y, ordered):
    order = one_hot(node_order(0, CELL), SIDE**3)
    ordered[...] = dot_columns(dot(order, stiffness[...]).astype(BF16), order)
    own_columns[...] = ordered[:, :OWN].astype(BF16)
    partial[...] = dot(own_columns[...], field[...])
    to_x, to_y = OWN, OWN + FACE
    own_x[...] = ordered[:OWN, to_x:to_y].astype(BF16)
    rim_x[...] = ordered[OWN : OWN + RIM, to_x:to_y].astype(BF16)
    face_x[...] = ordered[OWN + RIM :, to_x:to_y].astype(BF16)
    own_y[...] = ordered[:OWN, to_y:].astype(BF16)
    side_y[...] = ordered[OWN : OWN + FACE, to_y:].astype(BF16)
    face_y[...] = ordered[OWN + RIM :, to_y:].astype(BF16)
    edge_y[...] = ordered[OWN + FACE : OWN + RIM, to_y:].astype(BF16)


def cross(rim_x, face_x, partial, field, far_in, near_in, far, near, rim, above_x, raw, wide, face, upward, downward):
    def arrived(below, above):
        wide[...] = below[...].astype(F32)
        face[...] = above[:FACE, :].astype(F32)

    chosen(lax.axis_index("core") == 1, (far_in, near_in), arrived)
    above_x[...] = face[...].astype(BF16)
    rim[...] = wide[:RIM, :] + inside_x() * dot(rim_x[...], field[:FACE, :])
    row = partial[OWN + RIM :, :] + dot(face_x[...], above_x[...])
    downward[:DEG, :] = face[:DEG, :]
    stage_plane(field[...].astype(F32), downward, DEG)
    downward[RIM:, :] = wide[RIM:, :]
    wide[:FACE, :] = row
    wide[:DEG, :] += rim[FACE:, :]
    upward[...] = jnp.zeros_like(upward)
    stage_parts(wide[:FACE, :], upward)
    raw[...] = downward[...].astype(BF16)
    send(lax.bitwise_and(lax.axis_index("line"), 1) == 1, far, near, upward, downward)


def gather_row(own_x, face_y, edge_y, partial, field, above_x, rim, raw, own, corner, face):
    own[...] = partial[:OWN, :] + dot(own_x[...], above_x[...])
    own[:FACE, :] += rim[:FACE, :]
    face[...] = inside_y() * dot(face_y[...], raw[:RIM, :])
    for i in range(DEG):
        own[i * FACE : i * FACE + DEG, :] += face[i * DEG : (i + 1) * DEG, :]
    wide = raw[...].astype(F32)
    corner[:DEG, :] = field[...].astype(F32)[:DEG]
    corner[DEG:, :] = wide[RIM:]
    own[:DEG, :] += inside_x() * inside_y() * dot(edge_y[...], corner[...].astype(BF16))


def close(own_y, side_y, own, far_in, near_in, image, corner, face, wide):
    def arrived(below, above):
        parts = below[...].astype(F32)
        face[...] = parts[:FACE, :] + parts[FACE : 2 * FACE, :]
        wide[...] = above[...].astype(F32)

    chosen(lax.bitwise_and(lax.axis_index("line"), 1) == 1, (far_in, near_in), arrived)
    corner[:DEG, :] = wide[DEG : 2 * DEG, :]
    corner[DEG:, :] = wide[RIM:, :]
    image[:OWN, :] = own[...] + dot(own_y[...], wide[:RIM, :].astype(BF16))
    image[:FACE, :] += inside_x() * dot(side_y[...], corner[...].astype(BF16))
    for i in range(DEG):
        image[i * FACE : i * FACE + DEG, :] += face[i * DEG : (i + 1) * DEG, :]


def lift(
    own_y, side_y, own, far_in, near_in, field, potential, rim_own,
    lifted, far, near, image, corner, face, wide, upward,
):
    close(own_y, side_y, own, far_in, near_in, image, corner, face, wide)
    field32 = field[...].astype(F32)
    first_image = image[...] + potential[...] * field32
    image[...] = (first_image - SPECTRUM_CENTER * field32) / SPECTRUM_HALF
    lifted[...] = image[...].astype(BF16)
    pack_x(dot(rim_own[...], lifted[...]), image, far, near, upward, face)


def solution(mesh):
    length_x, length_y = mesh.shape["gx"], mesh.shape["gy"]
    length_z = length_x // 4
    length_row = max(1, length_y // 4)
    line = length_y // length_row
    split_mesh = Mesh(
        mesh.devices.reshape(length_z, 2, 2, length_row, line), ("z", "half", "core", "row", "line")
    )
    gx, gy = ("z", "half", "core"), ("row", "line")
    every = gx + gy

    def swapped(far, near, axis, length):
        def pairs(first):
            return [(i + j, i + 1 - j) for i in range(first, length - 1, 2) for j in range(2)]

        return lax.ppermute(far, axis, pairs(1)), lax.ppermute(near, axis, pairs(0))

    def per_device(orbitals, potential, cell_stiffness):
        node_count, orbital_count = orbitals.shape
        norm_scale = 1.0 / math.sqrt(node_count * length_x * length_y)
        block_rows = orbital_count // length_x
        block_cols = orbital_count // length_y
        half = orbital_count // 2
        quarter = orbital_count // 4
        padded = -(-OWN // 128) * 128

        def by_orbital(rows):
            return (rows, orbital_count)

        def staged(*rows):
            return tuple(pltpu.VMEM(by_orbital(n), F32) for n in rows)

        weight = potential[:, None]
        message_rows = RIM + FACE
        message = (by_orbital(message_rows), BF16)

        field, stiffness, rim_own, far, near = call(
            prepare,
            (by_orbital(OWN), BF16),
            ((SIDE**3, SIDE**3), BF16),
            ((RIM, OWN), BF16),
            message,
            message,
            scratch=(*staged(OWN, message_rows, FACE), pltpu.SemaphoreType.DMA((2,))),
            raw=(0, 1),
        )(orbitals, cell_stiffness)
        far, near = swapped(far, near, gx, length_x)
        own_columns, partial, own_x, rim_x, face_x, own_y, side_y, face_y, edge_y = call(
            arrange,
            ((CELL, OWN), BF16),
            (by_orbital(CELL), F32),
            ((OWN, FACE), BF16),
            ((RIM, FACE), BF16),
            ((FACE, FACE), BF16),
            ((OWN, RIM), BF16),
            ((FACE, RIM), BF16),
            ((FACE, RIM), BF16),
            ((DEG, RIM), BF16),
            scratch=(pltpu.VMEM((CELL, CELL), F32),),
        )(stiffness, field)

        def row_part(partial, values, far, near):
            far, near, rim, above_x, raw = call(
                cross,
                message,
                message,
                (by_orbital(RIM), F32),
                (by_orbital(FACE), BF16),
                message,
                scratch=staged(message_rows, FACE, message_rows, message_rows),
            )(rim_x, face_x, partial, values, far, near)
            far, near = swapped(far, near, gy, length_y)
            own = call(gather_row, (by_orbital(OWN), F32), scratch=staged(RIM, FACE))(
                own_x, face_y, edge_y, partial, values, above_x, rim, raw
            )[0]
            return own, far, near

        own, far, near = row_part(partial, field, far, near)
        lifted, far, near = call(
            lift,
            (by_orbital(OWN), BF16),
            message,
            message,
            scratch=staged(OWN, RIM, FACE, message_rows, message_rows),
        )(own_y, side_y, own, far, near, field, weight, rim_own)
        far, near = swapped(far, near, gx, length_x)

        def shuffle():
            place = lax.broadcasted_iota(jnp.int32, (orbital_count, 1), 0)
            line = lax.shift_right_logical(lax.bitwise_and(place, quarter - 1), block_rows.bit_length() - 1)
            side = lax.shift_right_logical(place, quarter.bit_length() - 1)
            core = lax.bitwise_xor(lax.shift_right_logical(side, 1), lax.axis_index("core"))
            block = line * 4 + lax.bitwise_and(side, 1) * 2 + core
            order = block * block_rows + lax.bitwise_and(place, block_rows - 1)
            return one_hot(order, orbital_count)

        def shuffled_product(own_columns, lifted, partial, order, shuffled):
            partial[...] = dot(own_columns[...], lifted[...])
            order[...] = shuffle()
            shuffled[...] = dot_columns(lifted[...], order[...]).astype(BF16)

        partial, order, shuffled = call(
            shuffled_product,
            (by_orbital(CELL), F32),
            ((orbital_count, orbital_count), BF16),
            (by_orbital(OWN), BF16),
        )(own_columns, lifted)
        own, far, near = row_part(partial, lifted, far, near)

        def filter_and_gram(
            own_y, side_y, own, far_in, near_in, field, lifted, potential, order, shuffled,
            filtered, keep, give, image, corner, face, wide, rows,
        ):
            def gram(which, left, right):
                product = (dot_rows(left, right) * norm_scale).astype(BF16)
                keep[which] = product[:, :half]
                give[which] = product[:, half:]

            close(own_y, side_y, own, far_in, near_in, image, corner, face, wide)
            image[OWN:, :] = jnp.zeros((padded - OWN, orbital_count), F32)
            rows[OWN:, :] = jnp.zeros((padded - OWN, orbital_count), F32)
            rows[:OWN, :] = shuffled[...].astype(F32)
            lifted32 = lifted[...].astype(F32)
            image[:OWN, :] += potential[...] * lifted32
            gram(0, image[...].astype(BF16), rows[...].astype(BF16))
            image[:OWN, :] = (
                2.0 * (image[:OWN, :] - SPECTRUM_CENTER * lifted32) / SPECTRUM_HALF - field[...].astype(F32)
            )
            filtered[...] = image[:OWN, :].astype(BF16)
            values = image[...].astype(BF16)
            gram(1, values, dot_columns(values, order[...]).astype(BF16))

        half_grams = ((2, orbital_count, half), BF16)
        filtered, kept, given = call(
            filter_and_gram,
            (by_orbital(OWN), BF16),
            half_grams,
            half_grams,
            scratch=staged(padded, RIM, FACE, message_rows, padded),
            results=(0,),
        )(own_y, side_y, own, far, near, field, lifted, weight, order, shuffled)
        taken = lax.ppermute(given, "core", [(0, 1), (1, 0)])

        def pair_sum(kept, taken, out):
            for which in range(2):
                total = (kept[which].astype(F32) + taken[which].astype(F32)).astype(BF16)
                for side in range(2):
                    part = total[:, side * quarter : (side + 1) * quarter]
                    for j in range(length_y):
                        out[j // line, side * line + j % line, which * block_cols : (which + 1) * block_cols] = part[
                            j * block_cols : (j + 1) * block_cols
                        ]

        def row_sum(terms, out):
            total = terms[0].astype(F32)
            for source in range(1, length_row):
                total += terms[source].astype(F32)
            out[...] = total.astype(BF16)

        wide = 2 * block_cols
        fold = max(1, 128 // wide)
        short = block_rows // fold

        def plane_sum(terms, out):
            total = terms[0].astype(F32)
            for source in range(1, 2 * line):
                total += terms[source].astype(F32)
            total = total.T.reshape(length_z, block_rows, wide)
            for part in range(fold):
                out[:, :, part * wide : (part + 1) * wide] = total[:, part * short : (part + 1) * short, :].astype(BF16)

        def line_sum(terms, ham, correlation):
            total = terms[0].astype(F32)
            for source in range(1, length_z):
                total += terms[source].astype(F32)
            for part in range(fold):
                block = total[:, part * wide : (part + 1) * wide]
                ham[part * short : (part + 1) * short, :] = block[:, :block_cols]
                correlation[part * short : (part + 1) * short, :] = block[:, block_cols:]

        terms = call(pair_sum, ((length_row, 2 * line, wide, quarter), BF16))(kept, taken)[0]
        terms = lax.all_to_all(terms, "row", 0, 0, tiled=True)
        terms = call(row_sum, ((2 * line, wide, quarter), BF16))(terms)[0]
        terms = lax.all_to_all(terms, ("half", "line"), 0, 0, tiled=True)
        terms = call(plane_sum, ((length_z, short, fold * wide), BF16))(terms)[0]
        terms = lax.all_to_all(terms, "z", 0, 0, tiled=True)
        block = (block_rows, block_cols)
        projected_ham, correlation = call(line_sum, (block, F32), (block, F32), results=(0, 1))(terms)
        return filtered, projected_ham, correlation

    return jax.shard_map(
        per_device,
        mesh=split_mesh,
        in_specs=(P(every, None), P(every), P()),
        out_specs=(P(every, None), P(gx, gy), P(gx, gy)),
        check_vma=False,
    )
```

```python
import math

import jax
import jax.numpy as jnp
from jax import lax
from jax.experimental import pallas as pl
from jax.experimental.pallas import tpu as pltpu
from jax.sharding import Mesh, PartitionSpec as P

DEG = 7
SIDE = DEG + 1
FACE = DEG * DEG
RIM = FACE + DEG
OWN = FACE * DEG
CELL = OWN + RIM + FACE
SPECTRUM_CENTER = 2.0
SPECTRUM_HALF = 2.0
VMEM_LIMIT = 24 * 2**20
F32 = jnp.float32
BF16 = jnp.bfloat16


def dot(left, right):
    return jnp.dot(left, right, preferred_element_type=F32)


def dot_rows(left, right):
    return lax.dot_general(left, right, (((0,), (0,)), ((), ())), preferred_element_type=F32)


def dot_columns(left, right):
    return lax.dot_general(left, right, (((1,), (1,)), ((), ())), preferred_element_type=F32)


def one_hot(column, width):
    return (column == lax.broadcasted_iota(jnp.int32, (column.shape[0], width), 1)).astype(F32).astype(BF16)


def node_order(first, count):
    place = first + lax.broadcasted_iota(jnp.int32, (count, 1), 0)

    def seventh(n):
        return lax.shift_right_logical(n * 9363, 16)

    column = seventh(place)
    plane = seventh(column)
    own = plane * SIDE * SIDE + (column - plane * DEG) * SIDE + (place - column * DEG)
    rim = place - OWN
    rim = DEG * SIDE * SIDE + seventh(rim) * SIDE + (rim - seventh(rim) * DEG)
    face = place - OWN - RIM
    face = seventh(face) * SIDE * SIDE + DEG * SIDE + (face - seventh(face) * DEG)
    return jnp.where(place < OWN, own, jnp.where(place < OWN + RIM, rim, face))


def call(kernel, *shapes, scratch=(), results=(), raw=()):
    def run(*args):
        vmem = pl.BlockSpec(memory_space=pltpu.VMEM)
        places = [
            pl.BlockSpec(memory_space=pl.ANY)
            if i in raw
            else vmem
            for i in range(len(args))
        ]
        return pl.pallas_call(
            kernel,
            out_shape=[
                jax.ShapeDtypeStruct(*shape) if i in results else pltpu.VMEM(*shape) for i, shape in enumerate(shapes)
            ],
            in_specs=places,
            out_specs=[vmem] * len(shapes),
            scratch_shapes=list(scratch),
            compiler_params=pltpu.CompilerParams(vmem_limit_bytes=VMEM_LIMIT),
            name=kernel.__name__,
        )(
            *[
                pltpu.with_memory_space_constraint(arg, pltpu.HBM if i in raw else pltpu.VMEM)
                for i, arg in enumerate(args)
            ]
        )

    return run


def chosen(upper, messages, arrived):
    far, near = messages

    @pl.when(upper)
    def _():
        arrived(near, far)

    @pl.when(jnp.logical_not(upper))
    def _():
        arrived(far, near)


def send(upper, far, near, upward, downward):
    @pl.when(upper)
    def _():
        far[...] = upward[...].astype(BF16)
        near[: downward.shape[0], :] = downward[...].astype(BF16)

    @pl.when(jnp.logical_not(upper))
    def _():
        near[...] = upward[...].astype(BF16)
        far[: downward.shape[0], :] = downward[...].astype(BF16)


def stage_parts(values, stage):
    count = values.shape[0]
    high = values.astype(BF16).astype(F32)
    stage[:count, :] = high
    stage[count : 2 * count, :] = values - high


def stage_plane(values, stage, start):
    for i in range(DEG):
        stage[start + i * DEG : start + (i + 1) * DEG, :] = values[i * FACE : i * FACE + DEG, :]


def pack_x(rim, wide, far, near, upward, downward):
    upward[:RIM, :] = rim
    stage_plane(wide, upward, RIM)
    downward[...] = wide[:FACE, :]
    send(lax.axis_index("core") == 1, far, near, upward, downward)


def inside_x():
    return (lax.axis_index("z") + lax.axis_index("half") + lax.axis_index("core") > 0).astype(F32)


def inside_y():
    return (lax.axis_index("gy") > 0).astype(F32)


def prepare(field_in, stiffness_in, field, stiffness, rim_own, far, near, wide, upward, downward, sems):
    top = DEG * SIDE * SIDE
    copies = [
        pltpu.make_async_copy(stiffness_in.at[top:], stiffness.at[top:], sems.at[0]),
        pltpu.make_async_copy(field_in, field, sems.at[1]),
        pltpu.make_async_copy(stiffness_in.at[:top], stiffness.at[:top], sems.at[2]),
    ]
    for copy in copies:
        copy.start()
    nodes = one_hot(node_order(0, OWN), SIDE**3)
    rim = one_hot(node_order(OWN, RIM) - top, SIDE * SIDE)
    copies[0].wait()
    rim_own[...] = dot_columns(dot(rim, stiffness[top:, :]).astype(BF16), nodes).astype(BF16)
    copies[1].wait()
    wide[...] = field[...].astype(F32)
    pack_x(dot(rim_own[...], field[...]), wide, far, near, upward, downward)
    copies[2].wait()


def arrange(stiffness, field, own_columns, partial, own_x, rim_x, face_x, own_y, side_y, face_y, edge_y, ordered):
    order = one_hot(node_order(0, CELL), SIDE**3)
    ordered[...] = dot_columns(dot(order, stiffness[...]).astype(BF16), order)
    own_columns[...] = ordered[:, :OWN].astype(BF16)
    partial[...] = dot(own_columns[...], field[...])
    to_x, to_y = OWN, OWN + FACE
    own_x[...] = ordered[:OWN, to_x:to_y].astype(BF16)
    rim_x[...] = ordered[OWN : OWN + RIM, to_x:to_y].astype(BF16)
    face_x[...] = ordered[OWN + RIM :, to_x:to_y].astype(BF16)
    own_y[...] = ordered[:OWN, to_y:].astype(BF16)
    side_y[...] = ordered[OWN : OWN + FACE, to_y:].astype(BF16)
    face_y[...] = ordered[OWN + RIM :, to_y:].astype(BF16)
    edge_y[...] = ordered[OWN + FACE : OWN + RIM, to_y:].astype(BF16)


def cross(rim_x, face_x, partial, field, far_in, near_in, far, near, rim, above_x, raw, wide, face, upward, downward):
    def arrived(below, above):
        wide[...] = below[...].astype(F32)
        face[...] = above[:FACE, :].astype(F32)

    chosen(lax.axis_index("core") == 1, (far_in, near_in), arrived)
    above_x[...] = face[...].astype(BF16)
    rim[...] = wide[:RIM, :] + inside_x() * dot(rim_x[...], field[:FACE, :])
    row = partial[OWN + RIM :, :] + dot(face_x[...], above_x[...])
    downward[:DEG, :] = face[:DEG, :]
    stage_plane(field[...].astype(F32), downward, DEG)
    downward[RIM:, :] = wide[RIM:, :]
    wide[:FACE, :] = row
    wide[:DEG, :] += rim[FACE:, :]
    upward[...] = jnp.zeros_like(upward)
    stage_parts(wide[:FACE, :], upward)
    raw[...] = downward[...].astype(BF16)
    send(lax.bitwise_and(lax.axis_index("gy"), 1) == 1, far, near, upward, downward)


def gather_row(own_x, face_y, edge_y, partial, field, above_x, rim, raw, own, corner, face):
    own[...] = partial[:OWN, :] + dot(own_x[...], above_x[...])
    own[:FACE, :] += rim[:FACE, :]
    face[...] = inside_y() * dot(face_y[...], raw[:RIM, :])
    for i in range(DEG):
        own[i * FACE : i * FACE + DEG, :] += face[i * DEG : (i + 1) * DEG, :]
    wide = raw[...].astype(F32)
    corner[:DEG, :] = field[...].astype(F32)[:DEG]
    corner[DEG:, :] = wide[RIM:]
    own[:DEG, :] += inside_x() * inside_y() * dot(edge_y[...], corner[...].astype(BF16))


def close(own_y, side_y, own, far_in, near_in, image, corner, face, wide):
    def arrived(below, above):
        parts = below[...].astype(F32)
        face[...] = parts[:FACE, :] + parts[FACE : 2 * FACE, :]
        wide[...] = above[...].astype(F32)

    chosen(lax.bitwise_and(lax.axis_index("gy"), 1) == 1, (far_in, near_in), arrived)
    corner[:DEG, :] = wide[DEG : 2 * DEG, :]
    corner[DEG:, :] = wide[RIM:, :]
    image[:OWN, :] = own[...] + dot(own_y[...], wide[:RIM, :].astype(BF16))
    image[:FACE, :] += inside_x() * dot(side_y[...], corner[...].astype(BF16))
    for i in range(DEG):
        image[i * FACE : i * FACE + DEG, :] += face[i * DEG : (i + 1) * DEG, :]


def lift(
    own_y, side_y, own, far_in, near_in, field, potential, rim_own,
    lifted, far, near, image, corner, face, wide, upward,
):
    close(own_y, side_y, own, far_in, near_in, image, corner, face, wide)
    field32 = field[...].astype(F32)
    first_image = image[...] + potential[...] * field32
    image[...] = (first_image - SPECTRUM_CENTER * field32) / SPECTRUM_HALF
    lifted[...] = image[...].astype(BF16)
    pack_x(dot(rim_own[...], lifted[...]), image, far, near, upward, face)


def solution(mesh):
    length_x, length_y = mesh.shape["gx"], mesh.shape["gy"]
    length_z = length_x // 4
    split_mesh = Mesh(mesh.devices.reshape(length_z, 2, 2, length_y), ("z", "half", "core", "gy"))
    gx = ("z", "half", "core")
    every = gx + ("gy",)

    def swapped(far, near, axis, length):
        def pairs(first):
            return [(i + j, i + 1 - j) for i in range(first, length - 1, 2) for j in range(2)]

        return lax.ppermute(far, axis, pairs(1)), lax.ppermute(near, axis, pairs(0))

    def per_device(orbitals, potential, cell_stiffness):
        node_count, orbital_count = orbitals.shape
        norm_scale = 1.0 / math.sqrt(node_count * length_x * length_y)
        block_rows = orbital_count // length_x
        block_cols = orbital_count // length_y
        half = orbital_count // 2
        quarter = orbital_count // 4
        padded = -(-OWN // 128) * 128

        def by_orbital(rows):
            return (rows, orbital_count)

        def staged(*rows):
            return tuple(pltpu.VMEM(by_orbital(n), F32) for n in rows)

        weight = potential[:, None]
        message_rows = RIM + FACE
        message = (by_orbital(message_rows), BF16)

        field, stiffness, rim_own, far, near = call(
            prepare,
            (by_orbital(OWN), BF16),
            ((SIDE**3, SIDE**3), BF16),
            ((RIM, OWN), BF16),
            message,
            message,
            scratch=(*staged(OWN, message_rows, FACE), pltpu.SemaphoreType.DMA((3,))),
            raw=(0, 1),
        )(orbitals, cell_stiffness)
        far, near = swapped(far, near, gx, length_x)
        own_columns, partial, own_x, rim_x, face_x, own_y, side_y, face_y, edge_y = call(
            arrange,
            ((CELL, OWN), BF16),
            (by_orbital(CELL), F32),
            ((OWN, FACE), BF16),
            ((RIM, FACE), BF16),
            ((FACE, FACE), BF16),
            ((OWN, RIM), BF16),
            ((FACE, RIM), BF16),
            ((FACE, RIM), BF16),
            ((DEG, RIM), BF16),
            scratch=(pltpu.VMEM((CELL, CELL), F32),),
        )(stiffness, field)

        def row_part(partial, values, far, near):
            far, near, rim, above_x, raw = call(
                cross,
                message,
                message,
                (by_orbital(RIM), F32),
                (by_orbital(FACE), BF16),
                message,
                scratch=staged(message_rows, FACE, message_rows, message_rows),
            )(rim_x, face_x, partial, values, far, near)
            far, near = swapped(far, near, "gy", length_y)
            own = call(gather_row, (by_orbital(OWN), F32), scratch=staged(RIM, FACE))(
                own_x, face_y, edge_y, partial, values, above_x, rim, raw
            )[0]
            return own, far, near

        own, far, near = row_part(partial, field, far, near)
        lifted, far, near = call(
            lift,
            (by_orbital(OWN), BF16),
            message,
            message,
            scratch=staged(OWN, RIM, FACE, message_rows, message_rows),
        )(own_y, side_y, own, far, near, field, weight, rim_own)
        far, near = swapped(far, near, gx, length_x)

        def shuffle():
            place = lax.broadcasted_iota(jnp.int32, (orbital_count, 1), 0)
            line = lax.shift_right_logical(lax.bitwise_and(place, quarter - 1), block_rows.bit_length() - 1)
            side = lax.shift_right_logical(place, quarter.bit_length() - 1)
            core = lax.bitwise_xor(lax.shift_right_logical(side, 1), lax.axis_index("core"))
            block = line * 4 + lax.bitwise_and(side, 1) * 2 + core
            order = block * block_rows + lax.bitwise_and(place, block_rows - 1)
            return one_hot(order, orbital_count)

        def shuffled_product(own_columns, lifted, partial, order, shuffled):
            partial[...] = dot(own_columns[...], lifted[...])
            order[...] = shuffle()
            shuffled[...] = dot_columns(lifted[...], order[...]).astype(BF16)

        partial, order, shuffled = call(
            shuffled_product,
            (by_orbital(CELL), F32),
            ((orbital_count, orbital_count), BF16),
            (by_orbital(OWN), BF16),
        )(own_columns, lifted)
        own, far, near = row_part(partial, lifted, far, near)

        def filter_and_gram(
            own_y, side_y, own, far_in, near_in, field, lifted, potential, order, shuffled,
            filtered, keep, give, image, corner, face, wide, rows,
        ):
            def gram(which, left, right):
                product = (dot_rows(left, right) * norm_scale).astype(BF16)
                keep[which] = product[:, :half]
                give[which] = product[:, half:]

            close(own_y, side_y, own, far_in, near_in, image, corner, face, wide)
            image[OWN:, :] = jnp.zeros((padded - OWN, orbital_count), F32)
            rows[OWN:, :] = jnp.zeros((padded - OWN, orbital_count), F32)
            rows[:OWN, :] = shuffled[...].astype(F32)
            lifted32 = lifted[...].astype(F32)
            image[:OWN, :] += potential[...] * lifted32
            gram(0, image[...].astype(BF16), rows[...].astype(BF16))
            image[:OWN, :] = (
                2.0 * (image[:OWN, :] - SPECTRUM_CENTER * lifted32) / SPECTRUM_HALF - field[...].astype(F32)
            )
            filtered[...] = image[:OWN, :].astype(BF16)
            values = image[...].astype(BF16)
            gram(1, values, dot_columns(values, order[...]).astype(BF16))

        half_grams = ((2, orbital_count, half), BF16)
        filtered, kept, given = call(
            filter_and_gram,
            (by_orbital(OWN), BF16),
            half_grams,
            half_grams,
            scratch=staged(padded, RIM, FACE, message_rows, padded),
            results=(0,),
        )(own_y, side_y, own, far, near, field, lifted, weight, order, shuffled)
        taken = lax.ppermute(given, "core", [(0, 1), (1, 0)])

        def pair_sum(kept, taken, out):
            for which in range(2):
                total = (kept[which].astype(F32) + taken[which].astype(F32)).astype(BF16)
                for side in range(2):
                    part = total[:, side * quarter : (side + 1) * quarter]
                    for j in range(length_y):
                        out[side, j, which * block_cols : (which + 1) * block_cols] = part[
                            j * block_cols : (j + 1) * block_cols
                        ]

        wide = 2 * block_cols
        fold = max(1, 128 // wide)
        short = block_rows // fold

        def plane_sum(terms, out):
            total = terms[0].astype(F32)
            for source in range(1, 2 * length_y):
                total += terms[source].astype(F32)
            total = total.T.reshape(length_z, block_rows, wide)
            for part in range(fold):
                out[:, :, part * wide : (part + 1) * wide] = total[:, part * short : (part + 1) * short, :].astype(BF16)

        def line_sum(terms, ham, correlation):
            total = terms[0].astype(F32)
            for source in range(1, length_z):
                total += terms[source].astype(F32)
            for part in range(fold):
                block = total[:, part * wide : (part + 1) * wide]
                ham[part * short : (part + 1) * short, :] = block[:, :block_cols]
                correlation[part * short : (part + 1) * short, :] = block[:, block_cols:]

        terms = call(pair_sum, ((2, length_y, wide, quarter), BF16))(kept, taken)[0]
        terms = terms.reshape(2 * length_y, wide, quarter)
        terms = lax.all_to_all(terms, ("half", "gy"), 0, 0, tiled=True)
        terms = call(plane_sum, ((length_z, short, fold * wide), BF16))(terms)[0]
        terms = lax.all_to_all(terms, "z", 0, 0, tiled=True)
        block = (block_rows, block_cols)
        projected_ham, correlation = call(line_sum, (block, F32), (block, F32), results=(0, 1))(terms)
        return filtered, projected_ham, correlation

    return jax.shard_map(
        per_device,
        mesh=split_mesh,
        in_specs=(P(every, None), P(every), P()),
        out_specs=(P(every, None), P(gx, "gy"), P(gx, "gy")),
        check_vma=False,
    )
```
